512 devices in a mesh: row: 32 (over y, x, core), col: 16 (over z).
Axes of the slice: x: 4, y: 4, z: 16, core: 2. Of those that a mesh axis runs over, the one named last changes fastest.
Arguments:
- kernel: bfloat16 [16, 32, 16, 16, 512], P(None, 'row', None, 'col'), as said below
Outputs:
- factor: float32 [16, 32, 16, 16, 512], P(None, 'row', None, 'col')
Inputs may be any that keep to these rules, and one draw needn't show every extreme that they name: kernel holds a symmetric positive definite matrix.
All inputs are finite; a program needn't handle non-finite values.
Results may differ from the reference program's by a relative error of at most 0.0046.
Values may be sent and summed in bfloat16 or wider, within the bound.
A program may use at most 64 MiB of HBM per device.

```python
import math
import jax
import jax.numpy as jnp
from jax import lax

P_SIZE = 512
NT = 16
BR = 16
BC = 32
TILE = 512
M = 8192
N_ROW = 32
N_COL = 16


SQRT_FIVE = 2.2360679775


def draw_kernel(key, part):
    matrix_order = NT * P_SIZE
    coord_key, weight_key, nugget_key = jax.random.split(key, 3)
    weights = jax.random.randint(weight_key, (8,), 1, 5).astype(jnp.float32)
    coords = jax.random.randint(coord_key, (matrix_order, 8), 0, 16).astype(jnp.float32)
    length = 16.0
    nugget_low = 0.05
    nugget_high = 0.2
    fraction = jax.random.uniform(nugget_key, (matrix_order,), jnp.float32, 0.0, 1.0)
    nugget = nugget_low * jnp.exp(fraction * math.log(nugget_high / nugget_low))
    diagonal_values = 1.0 + nugget
    positions = jnp.arange(matrix_order)

    def one_block(start_at):
        block_coords = lax.dynamic_slice_in_dim(coords, start_at, P_SIZE, 0)
        squared = jnp.zeros((P_SIZE, matrix_order), jnp.float32)
        for dim_at in range(8):
            gap_value = block_coords[:, dim_at][:, None] - coords[:, dim_at][None, :]
            squared = squared + weights[dim_at] * gap_value * gap_value
        scaled = jnp.sqrt(squared) * (SQRT_FIVE / length)
        values = (1.0 + scaled + scaled * scaled / 3.0) * jnp.exp(-scaled)
        on_diagonal = (start_at + jnp.arange(P_SIZE))[:, None] == positions[None, :]
        return jnp.where(on_diagonal, diagonal_values[None, :], values)
    blocks = lax.map(one_block, jnp.arange(NT) * P_SIZE)
    symmetric = blocks.reshape(matrix_order, matrix_order)
    tiled = symmetric.reshape(NT, N_ROW, BR, NT, N_COL, BC)
    return tiled.transpose(0, 1, 3, 4, 2, 5).reshape(NT, N_ROW, NT, N_COL, TILE).astype(jnp.bfloat16)


def setup_inputs(seed: int = 0) -> dict:
    key_list = jax.random.split(jax.random.key(seed), 2)
    kernel = draw_kernel(jax.random.fold_in(key_list[1], 71), 0)
    return dict(kernel=kernel)


def to_matrix(kernel):
    tiled = kernel.reshape(NT, N_ROW, NT, N_COL, BR, BC)
    return tiled.transpose(0, 1, 4, 2, 3, 5).reshape(M, M)

def to_tiles(matrix):
    tiled = matrix.reshape(NT, N_ROW, BR, NT, N_COL, BC)
    return tiled.transpose(0, 1, 3, 4, 2, 5).reshape(NT, N_ROW, NT, N_COL, TILE)

def reference(kernel):
    updated = to_matrix(kernel).astype(jnp.float32)
    result = jnp.zeros((M, M), jnp.float32)
    for panel_at in range(2):
        begin_at = panel_at * P_SIZE
        end_at = begin_at + P_SIZE
        corner_block = updated[begin_at:end_at, begin_at:end_at]
        corner_factor = jnp.linalg.cholesky(0.5 * (corner_block + corner_block.T))
        below_rows = updated[end_at:, begin_at:end_at]
        solved = jax.scipy.linalg.solve_triangular(corner_factor, below_rows.T, lower=True).T
        rounded = solved.astype(jnp.bfloat16)
        update_term = jnp.dot(rounded.astype(jnp.float32), rounded.T.astype(jnp.float32), preferred_element_type=jnp.float32)
        updated = updated.at[end_at:, end_at:].add(-update_term)
        result = result.at[begin_at:end_at, begin_at:end_at].set(corner_factor)
        result = result.at[end_at:, begin_at:end_at].set(solved)
    result = result.at[2 * P_SIZE:, 2 * P_SIZE:].set(updated[2 * P_SIZE:, 2 * P_SIZE:])
    return to_tiles(result)
```

```python
import jax
import jax.numpy as jnp
from jax import lax
from jax.sharding import PartitionSpec as P

P_SIZE = 512
NT = 16


def bf16_gram(left_side, right_side):
    return lax.dot_general(
        left_side.astype(jnp.bfloat16),
        right_side.astype(jnp.bfloat16),
        (((1,), (1,)), ((), ())),
        preferred_element_type=jnp.float32,
    )


def right_solve(factor, rows):
    return jax.scipy.linalg.solve_triangular(factor, rows.T, lower=True).T


def lower_factor(block):
    return jnp.linalg.cholesky(0.5 * (block + block.T))


def per_device(kernel):
    row_count = lax.axis_size("row")
    col_count = lax.axis_size("col")
    tile_rows = P_SIZE // row_count
    tile_cols = P_SIZE // col_count
    row_index = lax.axis_index("row")
    column_index = lax.axis_index("col")
    tiles = kernel.reshape(NT, NT, tile_rows, tile_cols)
    local = tiles.transpose(0, 2, 1, 3).reshape(NT * tile_rows, NT * tile_cols)

    with jax.named_scope("gather_inputs"):
        corner_tiles = jnp.stack([tiles[0, 0], tiles[1, 0], tiles[1, 1]])
        corners = lax.all_gather(corner_tiles, ("row", "col"), axis=0)
        corners = corners.reshape(row_count, col_count, 3, tile_rows, tile_cols)
        corners = corners.transpose(2, 0, 3, 1, 4).reshape(3, P_SIZE, P_SIZE)
        corners = corners.astype(jnp.float32)
        own_rows = lax.all_gather(local[tile_rows:, : 2 * tile_cols], "col", axis=0)
        own_rows = own_rows.reshape(col_count, (NT - 1) * tile_rows, 2, tile_cols)
        own_rows = own_rows.transpose(1, 2, 0, 3).reshape((NT - 1) * tile_rows, 2 * P_SIZE)
        own_rows = own_rows.astype(jnp.float32)
        col_rows = lax.all_gather(local[: 2 * tile_rows, tile_cols:], "row", axis=0)
        col_rows = col_rows.reshape(row_count, 2, tile_rows, (NT - 1) * tile_cols)
        col_rows = col_rows.transpose(3, 1, 0, 2).reshape((NT - 1) * tile_cols, 2 * P_SIZE)
        col_rows = col_rows.astype(jnp.float32)

    with jax.named_scope("first_panel"):
        first_factor = lower_factor(corners[0])
        own_count = (NT - 1) * tile_rows
        col_total = (NT - 1) * tile_cols
        stacked = jnp.concatenate(
            [corners[1], own_rows[:, :P_SIZE], col_rows[:, :P_SIZE]], axis=0
        )
        solved = right_solve(first_factor, stacked)
        next_rows = solved[:P_SIZE].astype(jnp.bfloat16)
        first_own = solved[P_SIZE : P_SIZE + own_count]
        first_col = solved[P_SIZE + own_count :]

    with jax.named_scope("second_panel"):
        second_corner = corners[2] - bf16_gram(next_rows, next_rows)
        second_factor = lower_factor(second_corner)
        own_below = own_rows[tile_rows:, P_SIZE:] - bf16_gram(first_own[tile_rows:], next_rows)
        col_below = col_rows[tile_cols:, P_SIZE:] - bf16_gram(first_col[tile_cols:], next_rows)
        solved = right_solve(second_factor, jnp.concatenate([own_below, col_below], axis=0))
        second_own = solved[: own_count - tile_rows]
        second_col = solved[own_count - tile_rows :]

    with jax.named_scope("trailing_update"):
        trailing = local[2 * tile_rows :, 2 * tile_cols :]
        trailing = trailing.astype(jnp.float32) - bf16_gram(
            first_own[tile_rows:], first_col[tile_cols:]
        )
        trailing = trailing - bf16_gram(second_own, second_col)

    with jax.named_scope("assemble"):
        start_row = row_index * tile_rows
        start_col = column_index * tile_cols
        first_corner = lax.dynamic_slice(first_factor, (start_row, start_col), (tile_rows, tile_cols))
        second_tile = lax.dynamic_slice(second_factor, (start_row, start_col), (tile_rows, tile_cols))
        first_cols = lax.dynamic_slice_in_dim(first_own, start_col, tile_cols, 1)
        second_cols = lax.dynamic_slice_in_dim(second_own, start_col, tile_cols, 1)
        result = jnp.zeros((NT * tile_rows, NT * tile_cols), jnp.float32)
        result = result.at[:tile_rows, :tile_cols].set(first_corner)
        result = result.at[tile_rows:, :tile_cols].set(first_cols)
        result = result.at[tile_rows : 2 * tile_rows, tile_cols : 2 * tile_cols].set(second_tile)
        result = result.at[2 * tile_rows :, tile_cols : 2 * tile_cols].set(second_cols)
        result = result.at[2 * tile_rows :, 2 * tile_cols :].set(trailing)
        result = result.reshape(NT, tile_rows, NT, tile_cols).transpose(0, 2, 1, 3)
    return result.reshape(NT, 1, NT, 1, tile_rows * tile_cols)


def solution(mesh):
    placed = (P(None, "row", None, "col", None),)
    return jax.shard_map(
        per_device,
        mesh=mesh,
        in_specs=placed,
        out_specs=P(None, "row", None, "col", None),
        check_vma=False,
    )
```

```python
import jax
import jax.numpy as jnp
from jax import lax
from jax.sharding import PartitionSpec as P

P_SIZE = 512
NT = 16


def bf16_gram(left_side, right_side):
    return lax.dot_general(
        left_side.astype(jnp.bfloat16),
        right_side.astype(jnp.bfloat16),
        (((1,), (1,)), ((), ())),
        preferred_element_type=jnp.float32,
    )


def right_solve(factor, rows):
    return jax.scipy.linalg.solve_triangular(factor, rows.T, lower=True).T


def lower_factor(block):
    return jnp.linalg.cholesky(0.5 * (block + block.T))


def per_device(kernel):
    row_count = lax.axis_size("row")
    col_count = lax.axis_size("col")
    tile_rows = P_SIZE // row_count
    tile_cols = P_SIZE // col_count
    row_index = lax.axis_index("row")
    column_index = lax.axis_index("col")
    tiles = kernel.reshape(NT, NT, tile_rows, tile_cols)
    local = tiles.transpose(0, 2, 1, 3).reshape(NT * tile_rows, NT * tile_cols)

    with jax.named_scope("gather_inputs"):
        corner_tiles = jnp.stack([tiles[0, 0], tiles[1, 0], tiles[1, 1]])
        corners = lax.all_gather(corner_tiles.reshape(1, -1), ("row", "col"), axis=0, tiled=True)
        corners = corners.reshape(row_count, col_count, 3, tile_rows, tile_cols)
        corners = corners.transpose(2, 0, 3, 1, 4).reshape(3, P_SIZE, P_SIZE)
        corners = corners.astype(jnp.float32)
        own_rows = lax.all_gather(local[tile_rows:, : 2 * tile_cols], "col", axis=0)
        own_rows = own_rows.reshape(col_count, (NT - 1) * tile_rows, 2, tile_cols)
        own_rows = own_rows.transpose(1, 2, 0, 3).reshape((NT - 1) * tile_rows, 2 * P_SIZE)
        own_rows = own_rows.astype(jnp.float32)
        col_rows = lax.all_gather(local[: 2 * tile_rows, tile_cols:], "row", axis=0)
        col_rows = col_rows.reshape(row_count, 2, tile_rows, (NT - 1) * tile_cols)
        col_rows = col_rows.transpose(3, 1, 0, 2).reshape((NT - 1) * tile_cols, 2 * P_SIZE)
        col_rows = col_rows.astype(jnp.float32)

    with jax.named_scope("first_panel"):
        first_factor = lower_factor(corners[0])
        own_count = (NT - 1) * tile_rows
        col_total = (NT - 1) * tile_cols
        stacked = jnp.concatenate(
            [corners[1], own_rows[:, :P_SIZE], col_rows[:, :P_SIZE]], axis=0
        )
        solved = right_solve(first_factor, stacked)
        next_rows = solved[:P_SIZE].astype(jnp.bfloat16)
        first_own = solved[P_SIZE : P_SIZE + own_count]
        first_col = solved[P_SIZE + own_count :]

    with jax.named_scope("second_panel"):
        second_corner = corners[2] - bf16_gram(next_rows, next_rows)
        second_factor = lower_factor(second_corner)
        own_below = own_rows[tile_rows:, P_SIZE:] - bf16_gram(first_own[tile_rows:], next_rows)
        col_below = col_rows[tile_cols:, P_SIZE:] - bf16_gram(first_col[tile_cols:], next_rows)
        solved = right_solve(second_factor, jnp.concatenate([own_below, col_below], axis=0))
        second_own = solved[: own_count - tile_rows]
        second_col = solved[own_count - tile_rows :]

    with jax.named_scope("trailing_update"):
        trailing = local[2 * tile_rows :, 2 * tile_cols :]
        trailing = trailing.astype(jnp.float32) - bf16_gram(
            first_own[tile_rows:], first_col[tile_cols:]
        )
        trailing = trailing - bf16_gram(second_own, second_col)

    with jax.named_scope("assemble"):
        start_row = row_index * tile_rows
        start_col = column_index * tile_cols
        first_corner = lax.dynamic_slice(first_factor, (start_row, start_col), (tile_rows, tile_cols))
        second_tile = lax.dynamic_slice(second_factor, (start_row, start_col), (tile_rows, tile_cols))
        first_cols = lax.dynamic_slice_in_dim(first_own, start_col, tile_cols, 1)
        second_cols = lax.dynamic_slice_in_dim(second_own, start_col, tile_cols, 1)
        result = jnp.zeros((NT * tile_rows, NT * tile_cols), jnp.float32)
        result = result.at[:tile_rows, :tile_cols].set(first_corner)
        result = result.at[tile_rows:, :tile_cols].set(first_cols)
        result = result.at[tile_rows : 2 * tile_rows, tile_cols : 2 * tile_cols].set(second_tile)
        result = result.at[2 * tile_rows :, tile_cols : 2 * tile_cols].set(second_cols)
        result = result.at[2 * tile_rows :, 2 * tile_cols :].set(trailing)
        result = result.reshape(NT, tile_rows, NT, tile_cols).transpose(0, 2, 1, 3)
    return result.reshape(NT, 1, NT, 1, tile_rows * tile_cols)


def solution(mesh):
    placed = (P(None, "row", None, "col", None),)
    return jax.shard_map(
        per_device,
        mesh=mesh,
        in_specs=placed,
        out_specs=P(None, "row", None, "col", None),
        check_vma=False,
    )
```

```python
import jax
import jax.numpy as jnp
from jax import lax
from jax.sharding import PartitionSpec as P

P_SIZE = 512
NT = 16


def bf16_gram(left_side, right_side):
    return lax.dot_general(
        left_side.astype(jnp.bfloat16),
        right_side.astype(jnp.bfloat16),
        (((1,), (1,)), ((), ())),
        preferred_element_type=jnp.float32,
    )


def right_solve(factor, rows):
    return jax.scipy.linalg.solve_triangular(factor, rows.T, lower=True).T


def lower_factor(block):
    return jnp.linalg.cholesky(0.5 * (block + block.T))


def per_device(kernel):
    row_count = lax.axis_size("row")
    col_count = lax.axis_size("col")
    tile_rows = P_SIZE // row_count
    tile_cols = P_SIZE // col_count
    row_index = lax.axis_index("row")
    column_index = lax.axis_index("col")
    tiles = kernel.reshape(NT, NT, tile_rows, tile_cols)
    local = tiles.transpose(0, 2, 1, 3).reshape(NT * tile_rows, NT * tile_cols)

    with jax.named_scope("gather_inputs"):
        band = lax.all_gather(local[:, : 2 * tile_cols], "col", axis=0)
        band = band.reshape(col_count, NT * tile_rows, 2, tile_cols)
        band = band.transpose(1, 2, 0, 3).reshape(NT * tile_rows, 2 * P_SIZE)
        own_rows = band[tile_rows:].astype(jnp.float32)
        top = jnp.concatenate([band[: 2 * tile_rows], local[: 2 * tile_rows, 2 * tile_cols :]], axis=1)
        top = lax.all_gather(top, "row", axis=0)
        top = top.reshape(row_count, 2, tile_rows, top.shape[-1]).transpose(1, 0, 2, 3)
        top = top.reshape(2 * P_SIZE, top.shape[-1]).astype(jnp.float32)
        corners = jnp.stack(
            [top[:P_SIZE, :P_SIZE], top[P_SIZE:, :P_SIZE], top[P_SIZE : 2 * P_SIZE, P_SIZE : 2 * P_SIZE]]
        )
        own_second = lax.dynamic_slice_in_dim(top, P_SIZE + column_index * tile_cols, tile_cols, 1)
        col_rows = jnp.concatenate([own_second, top[:, 2 * P_SIZE :]], axis=1).T

    with jax.named_scope("first_panel"):
        first_factor = lower_factor(corners[0])
        own_count = (NT - 1) * tile_rows
        col_total = (NT - 1) * tile_cols
        stacked = jnp.concatenate(
            [corners[1], own_rows[:, :P_SIZE], col_rows[:, :P_SIZE]], axis=0
        )
        solved = right_solve(first_factor, stacked)
        next_rows = solved[:P_SIZE].astype(jnp.bfloat16)
        first_own = solved[P_SIZE : P_SIZE + own_count]
        first_col = solved[P_SIZE + own_count :]

    with jax.named_scope("second_panel"):
        second_corner = corners[2] - bf16_gram(next_rows, next_rows)
        second_factor = lower_factor(second_corner)
        own_below = own_rows[tile_rows:, P_SIZE:] - bf16_gram(first_own[tile_rows:], next_rows)
        col_below = col_rows[tile_cols:, P_SIZE:] - bf16_gram(first_col[tile_cols:], next_rows)
        solved = right_solve(second_factor, jnp.concatenate([own_below, col_below], axis=0))
        second_own = solved[: own_count - tile_rows]
        second_col = solved[own_count - tile_rows :]

    with jax.named_scope("trailing_update"):
        trailing = local[2 * tile_rows :, 2 * tile_cols :]
        trailing = trailing.astype(jnp.float32) - bf16_gram(
            first_own[tile_rows:], first_col[tile_cols:]
        )
        trailing = trailing - bf16_gram(second_own, second_col)

    with jax.named_scope("assemble"):
        start_row = row_index * tile_rows
        start_col = column_index * tile_cols
        first_corner = lax.dynamic_slice(first_factor, (start_row, start_col), (tile_rows, tile_cols))
        second_tile = lax.dynamic_slice(second_factor, (start_row, start_col), (tile_rows, tile_cols))
        first_cols = lax.dynamic_slice_in_dim(first_own, start_col, tile_cols, 1)
        second_cols = lax.dynamic_slice_in_dim(second_own, start_col, tile_cols, 1)
        result = jnp.zeros((NT * tile_rows, NT * tile_cols), jnp.float32)
        result = result.at[:tile_rows, :tile_cols].set(first_corner)
        result = result.at[tile_rows:, :tile_cols].set(first_cols)
        result = result.at[tile_rows : 2 * tile_rows, tile_cols : 2 * tile_cols].set(second_tile)
        result = result.at[2 * tile_rows :, tile_cols : 2 * tile_cols].set(second_cols)
        result = result.at[2 * tile_rows :, 2 * tile_cols :].set(trailing)
        result = result.reshape(NT, tile_rows, NT, tile_cols).transpose(0, 2, 1, 3)
    return result.reshape(NT, 1, NT, 1, tile_rows * tile_cols)


def solution(mesh):
    placed = (P(None, "row", None, "col", None),)
    return jax.shard_map(
        per_device,
        mesh=mesh,
        in_specs=placed,
        out_specs=P(None, "row", None, "col", None),
        check_vma=False,
    )
```

```python
import jax
import jax.numpy as jnp
from jax import lax
from jax.experimental import pallas as pl
from jax.experimental.pallas import tpu as pltpu
from jax.sharding import PartitionSpec as P

P_SIZE = 512
NT = 16


def bf16_gram(left_side, right_side):
    return lax.dot_general(
        left_side.astype(jnp.bfloat16),
        right_side.astype(jnp.bfloat16),
        (((1,), (1,)), ((), ())),
        preferred_element_type=jnp.float32,
    )


BLOCK = 128
EXACT = lax.Precision.HIGHEST


def exact_dot(left_side, right_side):
    return lax.dot_general(
        left_side, right_side, (((1,), (1,)), ((), ())),
        precision=EXACT, preferred_element_type=jnp.float32,
    )


def factor_kernel(sym_ref, low_ref, inv_ref, work_ref, diag_ref, dinv_ref):
    size = sym_ref.shape[0]
    blocks = size // BLOCK
    work_ref[...] = sym_ref[...]
    low_ref[...] = jnp.zeros_like(low_ref)
    inv_ref[...] = jnp.zeros_like(inv_ref)
    rows = lax.broadcasted_iota(jnp.int32, (BLOCK, BLOCK), 0)
    lanes = lax.broadcasted_iota(jnp.int32, (BLOCK, BLOCK), 1)
    col_ids = lax.broadcasted_iota(jnp.int32, (BLOCK, 1), 0)
    row_ids = lax.broadcasted_iota(jnp.int32, (1, BLOCK), 1)
    eye = jnp.where(rows == lanes, 1.0, 0.0).astype(jnp.float32)
    for k in range(blocks):
        here = pl.ds(k * BLOCK, BLOCK)
        diag_ref[...] = jnp.zeros((BLOCK, BLOCK), jnp.float32)
        dinv_ref[...] = eye

        def step(j, block):
            col = jnp.sum(jnp.where(lanes == j, block, 0.0), axis=1, keepdims=True)
            row = jnp.sum(jnp.where(rows == j, block, 0.0), axis=0, keepdims=True)
            pivot = jnp.sum(jnp.where(col_ids == j, col, 0.0), axis=0, keepdims=True)
            root = jnp.sqrt(pivot)
            scale = 1.0 / root
            c_col = jnp.where(col_ids > j, col * scale, jnp.where(col_ids == j, root, 0.0))
            c_row = jnp.where(row_ids > j, row * scale, jnp.where(row_ids == j, root, 0.0))
            diag_ref[...] = jnp.where(lanes == j, c_col, diag_ref[...])
            inverse = dinv_ref[...]
            inv_row = jnp.sum(jnp.where(rows == j, inverse, 0.0), axis=0, keepdims=True)
            shift = jnp.where(col_ids == j, (root - 1.0) * scale, c_col * scale)
            dinv_ref[...] = inverse - shift * inv_row
            return block - c_col * c_row

        lax.fori_loop(0, BLOCK, step, work_ref[here, here])
        low_ref[here, here] = diag_ref[...]
        inv_ref[here, here] = dinv_ref[...]
        if k + 1 < blocks:
            rest = pl.ds((k + 1) * BLOCK, size - (k + 1) * BLOCK)
            panel = exact_dot(work_ref[rest, here], dinv_ref[...])
            low_ref[rest, here] = panel
            work_ref[rest, rest] = work_ref[rest, rest] - exact_dot(panel, panel)
    for i in range(1, blocks):
        at_i = pl.ds(i * BLOCK, BLOCK)
        for k in range(i):
            at_k = pl.ds(k * BLOCK, BLOCK)
            total = jnp.zeros((BLOCK, BLOCK), jnp.float32)
            for m in range(k, i):
                at_m = pl.ds(m * BLOCK, BLOCK)
                total = total + jnp.dot(
                    low_ref[at_i, at_m], inv_ref[at_m, at_k],
                    precision=EXACT, preferred_element_type=jnp.float32,
                )
            inv_ref[at_i, at_k] = -jnp.dot(
                inv_ref[at_i, at_i], total,
                precision=EXACT, preferred_element_type=jnp.float32,
            )


def factor_and_inverse(sym):
    size = sym.shape[0]
    return pl.pallas_call(
        factor_kernel,
        out_shape=(
            jax.ShapeDtypeStruct((size, size), jnp.float32),
            jax.ShapeDtypeStruct((size, size), jnp.float32),
        ),
        in_specs=[pl.BlockSpec(memory_space=pltpu.VMEM)],
        out_specs=(
            pl.BlockSpec(memory_space=pltpu.VMEM),
            pl.BlockSpec(memory_space=pltpu.VMEM),
        ),
        scratch_shapes=[
            pltpu.VMEM((size, size), jnp.float32),
            pltpu.VMEM((BLOCK, BLOCK), jnp.float32),
            pltpu.VMEM((BLOCK, BLOCK), jnp.float32),
        ],
    )(sym)


def per_device(kernel):
    row_count = lax.axis_size("row")
    col_count = lax.axis_size("col")
    tile_rows = P_SIZE // row_count
    tile_cols = P_SIZE // col_count
    row_index = lax.axis_index("row")
    column_index = lax.axis_index("col")
    tiles = kernel.reshape(NT, NT, tile_rows, tile_cols)
    local = tiles.transpose(0, 2, 1, 3).reshape(NT * tile_rows, NT * tile_cols)

    with jax.named_scope("gather_inputs"):
        band = lax.all_gather(local[:, : 2 * tile_cols], "col", axis=0)
        band = band.reshape(col_count, NT * tile_rows, 2, tile_cols)
        band = band.transpose(1, 2, 0, 3).reshape(NT * tile_rows, 2 * P_SIZE)
        own_rows = band[tile_rows:].astype(jnp.float32)
        top = jnp.concatenate([band[: 2 * tile_rows], local[: 2 * tile_rows, 2 * tile_cols :]], axis=1)
        top = lax.all_gather(top, "row", axis=0)
        top = top.reshape(row_count, 2, tile_rows, top.shape[-1]).transpose(1, 0, 2, 3)
        top = top.reshape(2 * P_SIZE, top.shape[-1]).astype(jnp.float32)
        corners = jnp.stack(
            [top[:P_SIZE, :P_SIZE], top[P_SIZE:, :P_SIZE], top[P_SIZE : 2 * P_SIZE, P_SIZE : 2 * P_SIZE]]
        )
        own_second = lax.dynamic_slice_in_dim(top, P_SIZE + column_index * tile_cols, tile_cols, 1)
        col_rows = jnp.concatenate([own_second, top[:, 2 * P_SIZE :]], axis=1).T

    with jax.named_scope("first_panel"):
        first_factor, first_inverse = factor_and_inverse(0.5 * (corners[0] + corners[0].T))
        own_count = (NT - 1) * tile_rows
        col_total = (NT - 1) * tile_cols
        stacked = jnp.concatenate(
            [corners[1], own_rows[:, :P_SIZE], col_rows[:, :P_SIZE]], axis=0
        )
        solved = exact_dot(stacked, first_inverse)
        next_rows = solved[:P_SIZE].astype(jnp.bfloat16)
        first_own = solved[P_SIZE : P_SIZE + own_count]
        first_col = solved[P_SIZE + own_count :]

    with jax.named_scope("second_panel"):
        second_corner = corners[2] - bf16_gram(next_rows, next_rows)
        second_factor, second_inverse = factor_and_inverse(0.5 * (second_corner + second_corner.T))
        own_below = own_rows[tile_rows:, P_SIZE:] - bf16_gram(first_own[tile_rows:], next_rows)
        col_below = col_rows[tile_cols:, P_SIZE:] - bf16_gram(first_col[tile_cols:], next_rows)
        solved = exact_dot(jnp.concatenate([own_below, col_below], axis=0), second_inverse)
        second_own = solved[: own_count - tile_rows]
        second_col = solved[own_count - tile_rows :]

    with jax.named_scope("trailing_update"):
        trailing = local[2 * tile_rows :, 2 * tile_cols :]
        trailing = trailing.astype(jnp.float32) - bf16_gram(
            first_own[tile_rows:], first_col[tile_cols:]
        )
        trailing = trailing - bf16_gram(second_own, second_col)

    with jax.named_scope("assemble"):
        start_row = row_index * tile_rows
        start_col = column_index * tile_cols
        first_corner = lax.dynamic_slice(first_factor, (start_row, start_col), (tile_rows, tile_cols))
        second_tile = lax.dynamic_slice(second_factor, (start_row, start_col), (tile_rows, tile_cols))
        first_cols = lax.dynamic_slice_in_dim(first_own, start_col, tile_cols, 1)
        second_cols = lax.dynamic_slice_in_dim(second_own, start_col, tile_cols, 1)
        result = jnp.zeros((NT * tile_rows, NT * tile_cols), jnp.float32)
        result = result.at[:tile_rows, :tile_cols].set(first_corner)
        result = result.at[tile_rows:, :tile_cols].set(first_cols)
        result = result.at[tile_rows : 2 * tile_rows, tile_cols : 2 * tile_cols].set(second_tile)
        result = result.at[2 * tile_rows :, tile_cols : 2 * tile_cols].set(second_cols)
        result = result.at[2 * tile_rows :, 2 * tile_cols :].set(trailing)
        result = result.reshape(NT, tile_rows, NT, tile_cols).transpose(0, 2, 1, 3)
    return result.reshape(NT, 1, NT, 1, tile_rows * tile_cols)


def solution(mesh):
    placed = (P(None, "row", None, "col", None),)
    return jax.shard_map(
        per_device,
        mesh=mesh,
        in_specs=placed,
        out_specs=P(None, "row", None, "col", None),
        check_vma=False,
    )
```

```python
import jax
import jax.numpy as jnp
from jax import lax
from jax.experimental import pallas as pl
from jax.experimental.pallas import tpu as pltpu
from jax.sharding import PartitionSpec as P

P_SIZE = 512
NT = 16


def bf16_gram(left_side, right_side):
    return lax.dot_general(
        left_side.astype(jnp.bfloat16),
        right_side.astype(jnp.bfloat16),
        (((1,), (1,)), ((), ())),
        preferred_element_type=jnp.float32,
    )


BLOCK = 128
EXACT = lax.Precision.HIGHEST


def exact_dot(left_side, right_side):
    return lax.dot_general(
        left_side, right_side, (((1,), (1,)), ((), ())),
        precision=EXACT, preferred_element_type=jnp.float32,
    )


def factor_kernel(sym_ref, low_ref, inv_ref, work_ref, diag_ref, dinv_ref):
    size = sym_ref.shape[0]
    blocks = size // BLOCK
    work_ref[...] = sym_ref[...]
    low_ref[...] = jnp.zeros_like(low_ref)
    inv_ref[...] = jnp.zeros_like(inv_ref)
    rows = lax.broadcasted_iota(jnp.int32, (BLOCK, BLOCK), 0)
    lanes = lax.broadcasted_iota(jnp.int32, (BLOCK, BLOCK), 1)
    col_ids = lax.broadcasted_iota(jnp.int32, (BLOCK, 1), 0)
    row_ids = lax.broadcasted_iota(jnp.int32, (1, BLOCK), 1)
    eye = jnp.where(rows == lanes, 1.0, 0.0).astype(jnp.float32)
    for k in range(blocks):
        here = pl.ds(k * BLOCK, BLOCK)
        diag_ref[...] = jnp.zeros((BLOCK, BLOCK), jnp.float32)
        dinv_ref[...] = eye

        def step(j, block):
            col = jnp.sum(jnp.where(lanes == j, block, 0.0), axis=1, keepdims=True)
            row = jnp.sum(jnp.where(rows == j, block, 0.0), axis=0, keepdims=True)
            pivot = jnp.sum(jnp.where(col_ids == j, col, 0.0), axis=0, keepdims=True)
            root = jnp.sqrt(pivot)
            scale = 1.0 / root
            c_col = jnp.where(col_ids > j, col * scale, jnp.where(col_ids == j, root, 0.0))
            c_row = jnp.where(row_ids > j, row * scale, jnp.where(row_ids == j, root, 0.0))
            diag_ref[...] = jnp.where(lanes == j, c_col, diag_ref[...])
            inverse = dinv_ref[...]
            inv_row = jnp.sum(jnp.where(rows == j, inverse, 0.0), axis=0, keepdims=True)
            shift = jnp.where(col_ids == j, (root - 1.0) * scale, c_col * scale)
            dinv_ref[...] = inverse - shift * inv_row
            return block - c_col * c_row

        lax.fori_loop(0, BLOCK, step, work_ref[here, here])
        low_ref[here, here] = diag_ref[...]
        inv_ref[here, here] = dinv_ref[...]
        if k + 1 < blocks:
            rest = pl.ds((k + 1) * BLOCK, size - (k + 1) * BLOCK)
            panel = exact_dot(work_ref[rest, here], dinv_ref[...])
            low_ref[rest, here] = panel
            work_ref[rest, rest] = work_ref[rest, rest] - exact_dot(panel, panel)
    for i in range(1, blocks):
        at_i = pl.ds(i * BLOCK, BLOCK)
        for k in range(i):
            at_k = pl.ds(k * BLOCK, BLOCK)
            total = jnp.zeros((BLOCK, BLOCK), jnp.float32)
            for m in range(k, i):
                at_m = pl.ds(m * BLOCK, BLOCK)
                total = total + jnp.dot(
                    low_ref[at_i, at_m], inv_ref[at_m, at_k],
                    precision=EXACT, preferred_element_type=jnp.float32,
                )
            inv_ref[at_i, at_k] = -jnp.dot(
                inv_ref[at_i, at_i], total,
                precision=EXACT, preferred_element_type=jnp.float32,
            )


def factor_and_inverse(sym):
    size = sym.shape[0]
    return pl.pallas_call(
        factor_kernel,
        out_shape=(
            jax.ShapeDtypeStruct((size, size), jnp.float32),
            jax.ShapeDtypeStruct((size, size), jnp.float32),
        ),
        in_specs=[pl.BlockSpec(memory_space=pltpu.VMEM)],
        out_specs=(
            pl.BlockSpec(memory_space=pltpu.VMEM),
            pl.BlockSpec(memory_space=pltpu.VMEM),
        ),
        scratch_shapes=[
            pltpu.VMEM((size, size), jnp.float32),
            pltpu.VMEM((BLOCK, BLOCK), jnp.float32),
            pltpu.VMEM((BLOCK, BLOCK), jnp.float32),
        ],
    )(sym)


def per_device(kernel):
    row_count = lax.axis_size("row")
    col_count = lax.axis_size("col")
    tile_rows = P_SIZE // row_count
    tile_cols = P_SIZE // col_count
    row_index = lax.axis_index("row")
    column_index = lax.axis_index("col")
    tiles = kernel.reshape(NT, NT, tile_rows, tile_cols)
    local = tiles.transpose(0, 2, 1, 3).reshape(NT * tile_rows, NT * tile_cols)

    with jax.named_scope("gather_corner"):
        corner_row = lax.all_gather(tiles[0, 0], "col", axis=1, tiled=True)
        corner = lax.all_gather(corner_row, "row", axis=0, tiled=True).astype(jnp.float32)

    with jax.named_scope("gather_inputs"):
        own_rows = lax.all_gather(local[tile_rows:, : 2 * tile_cols], "col", axis=0)
        own_rows = own_rows.reshape(col_count, (NT - 1) * tile_rows, 2, tile_cols)
        own_rows = own_rows.transpose(1, 2, 0, 3).reshape((NT - 1) * tile_rows, 2 * P_SIZE)
        next_band = lax.all_gather(own_rows[:tile_rows], "row", axis=0, tiled=True)
        own_rows = own_rows.astype(jnp.float32)
        next_band = next_band.astype(jnp.float32)
        col_rows = lax.all_gather(local[: 2 * tile_rows, tile_cols:], "row", axis=0)
        col_rows = col_rows.reshape(row_count, 2, tile_rows, (NT - 1) * tile_cols)
        col_rows = col_rows.transpose(3, 1, 0, 2).reshape((NT - 1) * tile_cols, 2 * P_SIZE)
        col_rows = col_rows.astype(jnp.float32)

    with jax.named_scope("first_panel"):
        first_factor, first_inverse = factor_and_inverse(0.5 * (corner + corner.T))
        own_count = (NT - 1) * tile_rows
        stacked = jnp.concatenate(
            [next_band[:, :P_SIZE], own_rows[:, :P_SIZE], col_rows[:, :P_SIZE]], axis=0
        )
        solved = exact_dot(stacked, first_inverse)
        next_rows = solved[:P_SIZE].astype(jnp.bfloat16)
        first_own = solved[P_SIZE : P_SIZE + own_count]
        first_col = solved[P_SIZE + own_count :]

    with jax.named_scope("second_panel"):
        second_corner = next_band[:, P_SIZE:] - bf16_gram(next_rows, next_rows)
        second_factor, second_inverse = factor_and_inverse(0.5 * (second_corner + second_corner.T))
        own_below = own_rows[tile_rows:, P_SIZE:] - bf16_gram(first_own[tile_rows:], next_rows)
        col_below = col_rows[tile_cols:, P_SIZE:] - bf16_gram(first_col[tile_cols:], next_rows)
        solved = exact_dot(jnp.concatenate([own_below, col_below], axis=0), second_inverse)
        second_own = solved[: own_count - tile_rows]
        second_col = solved[own_count - tile_rows :]

    with jax.named_scope("trailing_update"):
        trailing = local[2 * tile_rows :, 2 * tile_cols :]
        trailing = trailing.astype(jnp.float32) - bf16_gram(
            first_own[tile_rows:], first_col[tile_cols:]
        )
        trailing = trailing - bf16_gram(second_own, second_col)

    with jax.named_scope("assemble"):
        start_row = row_index * tile_rows
        start_col = column_index * tile_cols
        first_corner = lax.dynamic_slice(first_factor, (start_row, start_col), (tile_rows, tile_cols))
        second_tile = lax.dynamic_slice(second_factor, (start_row, start_col), (tile_rows, tile_cols))
        first_cols = lax.dynamic_slice_in_dim(first_own, start_col, tile_cols, 1)
        second_cols = lax.dynamic_slice_in_dim(second_own, start_col, tile_cols, 1)
        result = jnp.zeros((NT * tile_rows, NT * tile_cols), jnp.float32)
        result = result.at[:tile_rows, :tile_cols].set(first_corner)
        result = result.at[tile_rows:, :tile_cols].set(first_cols)
        result = result.at[tile_rows : 2 * tile_rows, tile_cols : 2 * tile_cols].set(second_tile)
        result = result.at[2 * tile_rows :, tile_cols : 2 * tile_cols].set(second_cols)
        result = result.at[2 * tile_rows :, 2 * tile_cols :].set(trailing)
        result = result.reshape(NT, tile_rows, NT, tile_cols).transpose(0, 2, 1, 3)
    return result.reshape(NT, 1, NT, 1, tile_rows * tile_cols)


def solution(mesh):
    placed = (P(None, "row", None, "col", None),)
    return jax.shard_map(
        per_device,
        mesh=mesh,
        in_specs=placed,
        out_specs=P(None, "row", None, "col", None),
        check_vma=False,
    )
```

```python
import functools
import jax
import jax.numpy as jnp
from jax import lax
from jax.experimental import pallas as pl
from jax.experimental.pallas import tpu as pltpu
from jax.sharding import PartitionSpec as P

P_SIZE = 512
NT = 16


def bf16_gram(left_side, right_side):
    return lax.dot_general(
        left_side.astype(jnp.bfloat16),
        right_side.astype(jnp.bfloat16),
        (((1,), (1,)), ((), ())),
        preferred_element_type=jnp.float32,
    )


BLOCK = 128
EXACT = lax.Precision.HIGHEST


def exact_dot(left_side, right_side):
    return lax.dot_general(
        left_side, right_side, (((1,), (1,)), ((), ())),
        precision=EXACT, preferred_element_type=jnp.float32,
    )


def factor_kernel(sym_ref, low_ref, inv_ref, work_ref, diag_ref, dinv_ref):
    size = sym_ref.shape[0]
    blocks = size // BLOCK
    work_ref[...] = sym_ref[...]
    low_ref[...] = jnp.zeros_like(low_ref)
    inv_ref[...] = jnp.zeros_like(inv_ref)
    rows = lax.broadcasted_iota(jnp.int32, (BLOCK, BLOCK), 0)
    lanes = lax.broadcasted_iota(jnp.int32, (BLOCK, BLOCK), 1)
    col_ids = lax.broadcasted_iota(jnp.int32, (BLOCK, 1), 0)
    row_ids = lax.broadcasted_iota(jnp.int32, (1, BLOCK), 1)
    eye = jnp.where(rows == lanes, 1.0, 0.0).astype(jnp.float32)
    for k in range(blocks):
        here = pl.ds(k * BLOCK, BLOCK)
        diag_ref[...] = jnp.zeros((BLOCK, BLOCK), jnp.float32)
        dinv_ref[...] = eye

        def step(j, block):
            col = jnp.sum(jnp.where(lanes == j, block, 0.0), axis=1, keepdims=True)
            row = jnp.sum(jnp.where(rows == j, block, 0.0), axis=0, keepdims=True)
            pivot = jnp.sum(jnp.where(col_ids == j, col, 0.0), axis=0, keepdims=True)
            root = jnp.sqrt(pivot)
            scale = 1.0 / root
            c_col = jnp.where(col_ids > j, col * scale, jnp.where(col_ids == j, root, 0.0))
            c_row = jnp.where(row_ids > j, row * scale, jnp.where(row_ids == j, root, 0.0))
            diag_ref[...] = jnp.where(lanes == j, c_col, diag_ref[...])
            inverse = dinv_ref[...]
            inv_row = jnp.sum(jnp.where(rows == j, inverse, 0.0), axis=0, keepdims=True)
            shift = jnp.where(col_ids == j, (root - 1.0) * scale, c_col * scale)
            dinv_ref[...] = inverse - shift * inv_row
            return block - c_col * c_row

        lax.fori_loop(0, BLOCK, step, work_ref[here, here])
        low_ref[here, here] = diag_ref[...]
        inv_ref[here, here] = dinv_ref[...]
        if k + 1 < blocks:
            rest = pl.ds((k + 1) * BLOCK, size - (k + 1) * BLOCK)
            panel = exact_dot(work_ref[rest, here], dinv_ref[...])
            low_ref[rest, here] = panel
            work_ref[rest, rest] = work_ref[rest, rest] - exact_dot(panel, panel)
    for i in range(1, blocks):
        at_i = pl.ds(i * BLOCK, BLOCK)
        for k in range(i):
            at_k = pl.ds(k * BLOCK, BLOCK)
            total = jnp.zeros((BLOCK, BLOCK), jnp.float32)
            for m in range(k, i):
                at_m = pl.ds(m * BLOCK, BLOCK)
                total = total + jnp.dot(
                    low_ref[at_i, at_m], inv_ref[at_m, at_k],
                    precision=EXACT, preferred_element_type=jnp.float32,
                )
            inv_ref[at_i, at_k] = -jnp.dot(
                inv_ref[at_i, at_i], total,
                precision=EXACT, preferred_element_type=jnp.float32,
            )


def factor_and_inverse(sym):
    size = sym.shape[0]
    return pl.pallas_call(
        factor_kernel,
        out_shape=(
            jax.ShapeDtypeStruct((size, size), jnp.float32),
            jax.ShapeDtypeStruct((size, size), jnp.float32),
        ),
        in_specs=[pl.BlockSpec(memory_space=pltpu.VMEM)],
        out_specs=(
            pl.BlockSpec(memory_space=pltpu.VMEM),
            pl.BlockSpec(memory_space=pltpu.VMEM),
        ),
        scratch_shapes=[
            pltpu.VMEM((size, size), jnp.float32),
            pltpu.VMEM((BLOCK, BLOCK), jnp.float32),
            pltpu.VMEM((BLOCK, BLOCK), jnp.float32),
        ],
    )(sym)


MESH_IDS = pl.DeviceIdType.MESH


def spread_kernel(axis, count, piece_ref, out_ref, send_sem, recv_sem):
    me = lax.axis_index(axis)
    barrier = pltpu.get_barrier_semaphore()
    for offset in range(1, count):
        peer = lax.rem(me + offset, count)
        pl.semaphore_signal(barrier, inc=1, device_id={axis: peer}, device_id_type=MESH_IDS)
    pl.semaphore_wait(barrier, count - 1)
    sends = []
    for offset in range(1, count):
        peer = lax.rem(me + offset, count)
        copy = pltpu.make_async_remote_copy(
            src_ref=piece_ref, dst_ref=out_ref.at[me],
            send_sem=send_sem.at[offset], recv_sem=recv_sem.at[offset],
            device_id={axis: peer}, device_id_type=MESH_IDS,
        )
        copy.start()
        sends.append(copy)
    out_ref[me] = piece_ref[...]
    for copy in sends:
        copy.wait_send()
    for offset in range(1, count):
        source = lax.rem(me + count - offset, count)
        arrival = pltpu.make_async_remote_copy(
            src_ref=piece_ref, dst_ref=out_ref.at[source],
            send_sem=send_sem.at[offset], recv_sem=recv_sem.at[offset],
            device_id={axis: source}, device_id_type=MESH_IDS,
        )
        arrival.wait_recv()


def spread(piece, axis, key):
    count = lax.axis_size(axis)
    return pl.pallas_call(
        functools.partial(spread_kernel, axis, count),
        out_shape=jax.ShapeDtypeStruct((count,) + piece.shape, piece.dtype),
        in_specs=[pl.BlockSpec(memory_space=pltpu.VMEM)],
        out_specs=pl.BlockSpec(memory_space=pltpu.VMEM),
        scratch_shapes=[pltpu.SemaphoreType.DMA((count,)), pltpu.SemaphoreType.DMA((count,))],
        compiler_params=pltpu.CompilerParams(collective_id=key, has_side_effects=True),
    )(piece)


def per_device(kernel):
    row_count = lax.axis_size("row")
    col_count = lax.axis_size("col")
    tile_rows = P_SIZE // row_count
    tile_cols = P_SIZE // col_count
    row_index = lax.axis_index("row")
    column_index = lax.axis_index("col")
    tiles = kernel.reshape(NT, NT, tile_rows, tile_cols)
    local = tiles.transpose(0, 2, 1, 3).reshape(NT * tile_rows, NT * tile_cols)

    with jax.named_scope("gather_inputs"):
        band = spread(local[:, : 2 * tile_cols], "col", 0)
        band = band.reshape(col_count, NT * tile_rows, 2, tile_cols)
        band = band.transpose(1, 2, 0, 3).reshape(NT * tile_rows, 2 * P_SIZE)
        own_rows = band[tile_rows:].astype(jnp.float32)
        top = jnp.concatenate([band[: 2 * tile_rows], local[: 2 * tile_rows, 2 * tile_cols :]], axis=1)
        top = spread(top, "row", 1)
        top = top.reshape(row_count, 2, tile_rows, top.shape[-1]).transpose(1, 0, 2, 3)
        top = top.reshape(2 * P_SIZE, top.shape[-1]).astype(jnp.float32)
        corners = jnp.stack(
            [top[:P_SIZE, :P_SIZE], top[P_SIZE:, :P_SIZE], top[P_SIZE : 2 * P_SIZE, P_SIZE : 2 * P_SIZE]]
        )
        own_second = lax.dynamic_slice_in_dim(top, P_SIZE + column_index * tile_cols, tile_cols, 1)
        col_rows = jnp.concatenate([own_second, top[:, 2 * P_SIZE :]], axis=1).T

    with jax.named_scope("first_panel"):
        first_factor, first_inverse = factor_and_inverse(0.5 * (corners[0] + corners[0].T))
        own_count = (NT - 1) * tile_rows
        col_total = (NT - 1) * tile_cols
        stacked = jnp.concatenate(
            [corners[1], own_rows[:, :P_SIZE], col_rows[:, :P_SIZE]], axis=0
        )
        solved = exact_dot(stacked, first_inverse)
        next_rows = solved[:P_SIZE].astype(jnp.bfloat16)
        first_own = solved[P_SIZE : P_SIZE + own_count]
        first_col = solved[P_SIZE + own_count :]

    with jax.named_scope("second_panel"):
        second_corner = corners[2] - bf16_gram(next_rows, next_rows)
        second_factor, second_inverse = factor_and_inverse(0.5 * (second_corner + second_corner.T))
        own_below = own_rows[tile_rows:, P_SIZE:] - bf16_gram(first_own[tile_rows:], next_rows)
        col_below = col_rows[tile_cols:, P_SIZE:] - bf16_gram(first_col[tile_cols:], next_rows)
        solved = exact_dot(jnp.concatenate([own_below, col_below], axis=0), second_inverse)
        second_own = solved[: own_count - tile_rows]
        second_col = solved[own_count - tile_rows :]

    with jax.named_scope("trailing_update"):
        trailing = local[2 * tile_rows :, 2 * tile_cols :]
        trailing = trailing.astype(jnp.float32) - bf16_gram(
            first_own[tile_rows:], first_col[tile_cols:]
        )
        trailing = trailing - bf16_gram(second_own, second_col)

    with jax.named_scope("assemble"):
        start_row = row_index * tile_rows
        start_col = column_index * tile_cols
        first_corner = lax.dynamic_slice(first_factor, (start_row, start_col), (tile_rows, tile_cols))
        second_tile = lax.dynamic_slice(second_factor, (start_row, start_col), (tile_rows, tile_cols))
        first_cols = lax.dynamic_slice_in_dim(first_own, start_col, tile_cols, 1)
        second_cols = lax.dynamic_slice_in_dim(second_own, start_col, tile_cols, 1)
        result = jnp.zeros((NT * tile_rows, NT * tile_cols), jnp.float32)
        result = result.at[:tile_rows, :tile_cols].set(first_corner)
        result = result.at[tile_rows:, :tile_cols].set(first_cols)
        result = result.at[tile_rows : 2 * tile_rows, tile_cols : 2 * tile_cols].set(second_tile)
        result = result.at[2 * tile_rows :, tile_cols : 2 * tile_cols].set(second_cols)
        result = result.at[2 * tile_rows :, 2 * tile_cols :].set(trailing)
        result = result.reshape(NT, tile_rows, NT, tile_cols).transpose(0, 2, 1, 3)
    return result.reshape(NT, 1, NT, 1, tile_rows * tile_cols)


def solution(mesh):
    placed = (P(None, "row", None, "col", None),)
    return jax.shard_map(
        per_device,
        mesh=mesh,
        in_specs=placed,
        out_specs=P(None, "row", None, "col", None),
        check_vma=False,
    )
```

```python
import jax
import jax.numpy as jnp
from jax import lax
from jax.experimental import pallas as pl
from jax.experimental.pallas import tpu as pltpu
from jax.sharding import PartitionSpec as P

P_SIZE = 512
NT = 16


def bf16_gram(left_side, right_side):
    return lax.dot_general(
        left_side.astype(jnp.bfloat16),
        right_side.astype(jnp.bfloat16),
        (((1,), (1,)), ((), ())),
        preferred_element_type=jnp.float32,
    )


BLOCK = 128
EXACT = lax.Precision.HIGHEST


def exact_dot(left_side, right_side):
    return lax.dot_general(
        left_side, right_side, (((1,), (1,)), ((), ())),
        precision=EXACT, preferred_element_type=jnp.float32,
    )


def factor_kernel(sym_ref, low_ref, inv_ref, work_ref, diag_ref, dinv_ref):
    size = sym_ref.shape[0]
    blocks = size // BLOCK
    work_ref[...] = sym_ref[...]
    low_ref[...] = jnp.zeros_like(low_ref)
    inv_ref[...] = jnp.zeros_like(inv_ref)
    rows = lax.broadcasted_iota(jnp.int32, (BLOCK, BLOCK), 0)
    lanes = lax.broadcasted_iota(jnp.int32, (BLOCK, BLOCK), 1)
    col_ids = lax.broadcasted_iota(jnp.int32, (BLOCK, 1), 0)
    row_ids = lax.broadcasted_iota(jnp.int32, (1, BLOCK), 1)
    eye = jnp.where(rows == lanes, 1.0, 0.0).astype(jnp.float32)
    for k in range(blocks):
        here = pl.ds(k * BLOCK, BLOCK)
        diag_ref[...] = jnp.zeros((BLOCK, BLOCK), jnp.float32)
        dinv_ref[...] = eye

        def pick_col(block, at):
            return jnp.sum(jnp.where(lanes == at, block, 0.0), axis=1, keepdims=True)

        def pick_row(block, at):
            return jnp.sum(jnp.where(rows == at, block, 0.0), axis=0, keepdims=True)

        def entry(vector, at):
            return jnp.sum(jnp.where(col_ids == at, vector, 0.0), axis=0, keepdims=True)

        def step(half, block):
            j = 2 * half
            k = j + 1
            col_j = pick_col(block, j)
            col_k = pick_col(block, k)
            row_j = pick_row(block, j)
            row_k = pick_row(block, k)
            root_j = jnp.sqrt(entry(col_j, j))
            scale_j = 1.0 / root_j
            cross = entry(col_j, k) * scale_j
            root_k = jnp.sqrt(entry(col_k, k) - cross * cross)
            scale_k = 1.0 / root_k
            c_col_j = jnp.where(col_ids > j, col_j * scale_j, jnp.where(col_ids == j, root_j, 0.0))
            c_row_j = jnp.where(row_ids > j, row_j * scale_j, jnp.where(row_ids == j, root_j, 0.0))
            c_col_k = jnp.where(
                col_ids > k, (col_k - c_col_j * cross) * scale_k, jnp.where(col_ids == k, root_k, 0.0)
            )
            c_row_k = jnp.where(
                row_ids > k, (row_k - c_row_j * cross) * scale_k, jnp.where(row_ids == k, root_k, 0.0)
            )
            diag_ref[...] = jnp.where(
                lanes == j, c_col_j, jnp.where(lanes == k, c_col_k, diag_ref[...])
            )
            inverse = dinv_ref[...]
            shift_j = c_col_j * scale_j - jnp.where(col_ids == j, scale_j, 0.0)
            inverse = inverse - shift_j * pick_row(inverse, j)
            shift_k = c_col_k * scale_k - jnp.where(col_ids == k, scale_k, 0.0)
            dinv_ref[...] = inverse - shift_k * pick_row(inverse, k)
            return block - c_col_j * c_row_j - c_col_k * c_row_k

        lax.fori_loop(0, BLOCK // 2, step, work_ref[here, here], unroll=2)
        low_ref[here, here] = diag_ref[...]
        inv_ref[here, here] = dinv_ref[...]
        if k + 1 < blocks:
            rest = pl.ds((k + 1) * BLOCK, size - (k + 1) * BLOCK)
            panel = exact_dot(work_ref[rest, here], dinv_ref[...])
            low_ref[rest, here] = panel
            work_ref[rest, rest] = work_ref[rest, rest] - exact_dot(panel, panel)
    for i in range(1, blocks):
        at_i = pl.ds(i * BLOCK, BLOCK)
        for k in range(i):
            at_k = pl.ds(k * BLOCK, BLOCK)
            total = jnp.zeros((BLOCK, BLOCK), jnp.float32)
            for m in range(k, i):
                at_m = pl.ds(m * BLOCK, BLOCK)
                total = total + jnp.dot(
                    low_ref[at_i, at_m], inv_ref[at_m, at_k],
                    precision=EXACT, preferred_element_type=jnp.float32,
                )
            inv_ref[at_i, at_k] = -jnp.dot(
                inv_ref[at_i, at_i], total,
                precision=EXACT, preferred_element_type=jnp.float32,
            )


def factor_and_inverse(sym):
    size = sym.shape[0]
    return pl.pallas_call(
        factor_kernel,
        out_shape=(
            jax.ShapeDtypeStruct((size, size), jnp.float32),
            jax.ShapeDtypeStruct((size, size), jnp.float32),
        ),
        in_specs=[pl.BlockSpec(memory_space=pltpu.VMEM)],
        out_specs=(
            pl.BlockSpec(memory_space=pltpu.VMEM),
            pl.BlockSpec(memory_space=pltpu.VMEM),
        ),
        scratch_shapes=[
            pltpu.VMEM((size, size), jnp.float32),
            pltpu.VMEM((BLOCK, BLOCK), jnp.float32),
            pltpu.VMEM((BLOCK, BLOCK), jnp.float32),
        ],
    )(sym)


def per_device(kernel):
    row_count = lax.axis_size("row")
    col_count = lax.axis_size("col")
    tile_rows = P_SIZE // row_count
    tile_cols = P_SIZE // col_count
    row_index = lax.axis_index("row")
    column_index = lax.axis_index("col")
    tiles = kernel.reshape(NT, NT, tile_rows, tile_cols)
    local = tiles.transpose(0, 2, 1, 3).reshape(NT * tile_rows, NT * tile_cols)

    with jax.named_scope("gather_inputs"):
        band = lax.all_gather(local[:, : 2 * tile_cols], "col", axis=0)
        band = band.reshape(col_count, NT * tile_rows, 2, tile_cols)
        band = band.transpose(1, 2, 0, 3).reshape(NT * tile_rows, 2 * P_SIZE)
        own_rows = band[tile_rows:].astype(jnp.float32)
        top = jnp.concatenate([band[: 2 * tile_rows], local[: 2 * tile_rows, 2 * tile_cols :]], axis=1)
        top = lax.all_gather(top, "row", axis=0)
        top = top.reshape(row_count, 2, tile_rows, top.shape[-1]).transpose(1, 0, 2, 3)
        top = top.reshape(2 * P_SIZE, top.shape[-1]).astype(jnp.float32)
        corners = jnp.stack(
            [top[:P_SIZE, :P_SIZE], top[P_SIZE:, :P_SIZE], top[P_SIZE : 2 * P_SIZE, P_SIZE : 2 * P_SIZE]]
        )
        own_second = lax.dynamic_slice_in_dim(top, P_SIZE + column_index * tile_cols, tile_cols, 1)
        col_rows = jnp.concatenate([own_second, top[:, 2 * P_SIZE :]], axis=1).T

    with jax.named_scope("first_panel"):
        first_factor, first_inverse = factor_and_inverse(0.5 * (corners[0] + corners[0].T))
        own_count = (NT - 1) * tile_rows
        col_total = (NT - 1) * tile_cols
        stacked = jnp.concatenate(
            [corners[1], own_rows[:, :P_SIZE], col_rows[:, :P_SIZE]], axis=0
        )
        solved = exact_dot(stacked, first_inverse)
        next_rows = solved[:P_SIZE].astype(jnp.bfloat16)
        first_own = solved[P_SIZE : P_SIZE + own_count]
        first_col = solved[P_SIZE + own_count :]

    with jax.named_scope("second_panel"):
        second_corner = corners[2] - bf16_gram(next_rows, next_rows)
        second_factor, second_inverse = factor_and_inverse(0.5 * (second_corner + second_corner.T))
        own_below = own_rows[tile_rows:, P_SIZE:] - bf16_gram(first_own[tile_rows:], next_rows)
        col_below = col_rows[tile_cols:, P_SIZE:] - bf16_gram(first_col[tile_cols:], next_rows)
        solved = exact_dot(jnp.concatenate([own_below, col_below], axis=0), second_inverse)
        second_own = solved[: own_count - tile_rows]
        second_col = solved[own_count - tile_rows :]

    with jax.named_scope("trailing_update"):
        trailing = local[2 * tile_rows :, 2 * tile_cols :]
        trailing = trailing.astype(jnp.float32) - bf16_gram(
            first_own[tile_rows:], first_col[tile_cols:]
        )
        trailing = trailing - bf16_gram(second_own, second_col)

    with jax.named_scope("assemble"):
        start_row = row_index * tile_rows
        start_col = column_index * tile_cols
        first_corner = lax.dynamic_slice(first_factor, (start_row, start_col), (tile_rows, tile_cols))
        second_tile = lax.dynamic_slice(second_factor, (start_row, start_col), (tile_rows, tile_cols))
        first_cols = lax.dynamic_slice_in_dim(first_own, start_col, tile_cols, 1)
        second_cols = lax.dynamic_slice_in_dim(second_own, start_col, tile_cols, 1)
        result = jnp.zeros((NT * tile_rows, NT * tile_cols), jnp.float32)
        result = result.at[:tile_rows, :tile_cols].set(first_corner)
        result = result.at[tile_rows:, :tile_cols].set(first_cols)
        result = result.at[tile_rows : 2 * tile_rows, tile_cols : 2 * tile_cols].set(second_tile)
        result = result.at[2 * tile_rows :, tile_cols : 2 * tile_cols].set(second_cols)
        result = result.at[2 * tile_rows :, 2 * tile_cols :].set(trailing)
        result = result.reshape(NT, tile_rows, NT, tile_cols).transpose(0, 2, 1, 3)
    return result.reshape(NT, 1, NT, 1, tile_rows * tile_cols)


def solution(mesh):
    placed = (P(None, "row", None, "col", None),)
    return jax.shard_map(
        per_device,
        mesh=mesh,
        in_specs=placed,
        out_specs=P(None, "row", None, "col", None),
        check_vma=False,
    )
```

```python
import jax
import jax.numpy as jnp
from jax import lax
from jax.experimental import pallas as pl
from jax.experimental.pallas import tpu as pltpu
from jax.sharding import PartitionSpec as P

P_SIZE = 512
NT = 16


def bf16_gram(left_side, right_side):
    return lax.dot_general(
        left_side.astype(jnp.bfloat16),
        right_side.astype(jnp.bfloat16),
        (((1,), (1,)), ((), ())),
        preferred_element_type=jnp.float32,
    )


BLOCK = 128
EXACT = lax.Precision.HIGHEST


def exact_dot(left_side, right_side):
    return lax.dot_general(
        left_side, right_side, (((1,), (1,)), ((), ())),
        precision=EXACT, preferred_element_type=jnp.float32,
    )


def factor_kernel(sym_ref, low_ref, inv_ref, work_ref, diag_ref, dinv_ref):
    size = sym_ref.shape[0]
    blocks = size // BLOCK
    work_ref[...] = sym_ref[...]
    low_ref[...] = jnp.zeros_like(low_ref)
    inv_ref[...] = jnp.zeros_like(inv_ref)
    rows = lax.broadcasted_iota(jnp.int32, (BLOCK, BLOCK), 0)
    lanes = lax.broadcasted_iota(jnp.int32, (BLOCK, BLOCK), 1)
    col_ids = lax.broadcasted_iota(jnp.int32, (BLOCK, 1), 0)
    row_ids = lax.broadcasted_iota(jnp.int32, (1, BLOCK), 1)
    eye = jnp.where(rows == lanes, 1.0, 0.0).astype(jnp.float32)
    for k in range(blocks):
        here = pl.ds(k * BLOCK, BLOCK)
        diag_ref[...] = jnp.zeros((BLOCK, BLOCK), jnp.float32)
        dinv_ref[...] = eye

        def pick_col(block, at):
            return jnp.sum(jnp.where(lanes == at, block, 0.0), axis=1, keepdims=True)

        def pick_row(block, at):
            return jnp.sum(jnp.where(rows == at, block, 0.0), axis=0, keepdims=True)

        def entry(vector, at):
            return jnp.sum(jnp.where(col_ids == at, vector, 0.0), axis=0, keepdims=True)

        def step(half, block):
            j = 2 * half
            k = j + 1
            col_j = pick_col(block, j)
            col_k = pick_col(block, k)
            row_j = pick_row(block, j)
            row_k = pick_row(block, k)
            root_j = jnp.sqrt(entry(col_j, j))
            scale_j = 1.0 / root_j
            cross = entry(col_j, k) * scale_j
            root_k = jnp.sqrt(entry(col_k, k) - cross * cross)
            scale_k = 1.0 / root_k
            c_col_j = jnp.where(col_ids > j, col_j * scale_j, jnp.where(col_ids == j, root_j, 0.0))
            c_row_j = jnp.where(row_ids > j, row_j * scale_j, jnp.where(row_ids == j, root_j, 0.0))
            c_col_k = jnp.where(
                col_ids > k, (col_k - c_col_j * cross) * scale_k, jnp.where(col_ids == k, root_k, 0.0)
            )
            c_row_k = jnp.where(
                row_ids > k, (row_k - c_row_j * cross) * scale_k, jnp.where(row_ids == k, root_k, 0.0)
            )
            diag_ref[...] = jnp.where(
                lanes == j, c_col_j, jnp.where(lanes == k, c_col_k, diag_ref[...])
            )
            inverse = dinv_ref[...]
            shift_j = c_col_j * scale_j - jnp.where(col_ids == j, scale_j, 0.0)
            inverse = inverse - shift_j * pick_row(inverse, j)
            shift_k = c_col_k * scale_k - jnp.where(col_ids == k, scale_k, 0.0)
            dinv_ref[...] = inverse - shift_k * pick_row(inverse, k)
            return block - c_col_j * c_row_j - c_col_k * c_row_k

        lax.fori_loop(0, BLOCK // 2, step, work_ref[here, here], unroll=2)
        low_ref[here, here] = diag_ref[...]
        inv_ref[here, here] = dinv_ref[...]
        if k + 1 < blocks:
            rest = pl.ds((k + 1) * BLOCK, size - (k + 1) * BLOCK)
            panel = exact_dot(work_ref[rest, here], dinv_ref[...])
            low_ref[rest, here] = panel
            work_ref[rest, rest] = work_ref[rest, rest] - exact_dot(panel, panel)
    for i in range(1, blocks):
        at_i = pl.ds(i * BLOCK, BLOCK)
        for k in range(i):
            at_k = pl.ds(k * BLOCK, BLOCK)
            total = jnp.zeros((BLOCK, BLOCK), jnp.float32)
            for m in range(k, i):
                at_m = pl.ds(m * BLOCK, BLOCK)
                total = total + jnp.dot(
                    low_ref[at_i, at_m], inv_ref[at_m, at_k],
                    precision=EXACT, preferred_element_type=jnp.float32,
                )
            inv_ref[at_i, at_k] = -jnp.dot(
                inv_ref[at_i, at_i], total,
                precision=EXACT, preferred_element_type=jnp.float32,
            )


def factor_and_inverse(sym):
    size = sym.shape[0]
    return pl.pallas_call(
        factor_kernel,
        out_shape=(
            jax.ShapeDtypeStruct((size, size), jnp.float32),
            jax.ShapeDtypeStruct((size, size), jnp.float32),
        ),
        in_specs=[pl.BlockSpec(memory_space=pltpu.VMEM)],
        out_specs=(
            pl.BlockSpec(memory_space=pltpu.VMEM),
            pl.BlockSpec(memory_space=pltpu.VMEM),
        ),
        scratch_shapes=[
            pltpu.VMEM((size, size), jnp.float32),
            pltpu.VMEM((BLOCK, BLOCK), jnp.float32),
            pltpu.VMEM((BLOCK, BLOCK), jnp.float32),
        ],
    )(sym)


def per_device(kernel):
    row_count = lax.axis_size("row")
    col_count = lax.axis_size("col")
    tile_rows = P_SIZE // row_count
    tile_cols = P_SIZE // col_count
    row_index = lax.axis_index("row")
    column_index = lax.axis_index("col")
    tiles = kernel.reshape(NT, NT, tile_rows, tile_cols)
    local = tiles.transpose(0, 2, 1, 3).reshape(NT * tile_rows, NT * tile_cols)

    with jax.named_scope("gather_inputs"):
        band = lax.all_gather(local[:, : 2 * tile_cols], "col", axis=0)
        band = band.reshape(col_count, NT * tile_rows, 2, tile_cols)
        band = band.transpose(1, 2, 0, 3).reshape(NT * tile_rows, 2 * P_SIZE)
        own_rows = band[tile_rows:].astype(jnp.float32)
        corner = lax.all_gather(band[:tile_rows, :P_SIZE], "row", axis=0, tiled=True)
        corner = corner.astype(jnp.float32)
        top = jnp.concatenate([band[: 2 * tile_rows], local[: 2 * tile_rows, 2 * tile_cols :]], axis=1)
        top = lax.all_gather(top, "row", axis=0)
        top = top.reshape(row_count, 2, tile_rows, top.shape[-1]).transpose(1, 0, 2, 3)
        top = top.reshape(2 * P_SIZE, top.shape[-1]).astype(jnp.float32)
        corners = jnp.stack([top[P_SIZE:, :P_SIZE], top[P_SIZE : 2 * P_SIZE, P_SIZE : 2 * P_SIZE]])
        own_second = lax.dynamic_slice_in_dim(top, P_SIZE + column_index * tile_cols, tile_cols, 1)
        col_rows = jnp.concatenate([own_second, top[:, 2 * P_SIZE :]], axis=1).T

    with jax.named_scope("first_panel"):
        first_factor, first_inverse = factor_and_inverse(0.5 * (corner + corner.T))
        own_count = (NT - 1) * tile_rows
        col_total = (NT - 1) * tile_cols
        stacked = jnp.concatenate(
            [corners[0], own_rows[:, :P_SIZE], col_rows[:, :P_SIZE]], axis=0
        )
        solved = exact_dot(stacked, first_inverse)
        next_rows = solved[:P_SIZE].astype(jnp.bfloat16)
        first_own = solved[P_SIZE : P_SIZE + own_count]
        first_col = solved[P_SIZE + own_count :]

    with jax.named_scope("second_panel"):
        second_corner = corners[1] - bf16_gram(next_rows, next_rows)
        second_factor, second_inverse = factor_and_inverse(0.5 * (second_corner + second_corner.T))
        own_below = own_rows[tile_rows:, P_SIZE:] - bf16_gram(first_own[tile_rows:], next_rows)
        col_below = col_rows[tile_cols:, P_SIZE:] - bf16_gram(first_col[tile_cols:], next_rows)
        solved = exact_dot(jnp.concatenate([own_below, col_below], axis=0), second_inverse)
        second_own = solved[: own_count - tile_rows]
        second_col = solved[own_count - tile_rows :]

    with jax.named_scope("trailing_update"):
        trailing = local[2 * tile_rows :, 2 * tile_cols :]
        trailing = trailing.astype(jnp.float32) - bf16_gram(
            first_own[tile_rows:], first_col[tile_cols:]
        )
        trailing = trailing - bf16_gram(second_own, second_col)

    with jax.named_scope("assemble"):
        start_row = row_index * tile_rows
        start_col = column_index * tile_cols
        first_corner = lax.dynamic_slice(first_factor, (start_row, start_col), (tile_rows, tile_cols))
        second_tile = lax.dynamic_slice(second_factor, (start_row, start_col), (tile_rows, tile_cols))
        first_cols = lax.dynamic_slice_in_dim(first_own, start_col, tile_cols, 1)
        second_cols = lax.dynamic_slice_in_dim(second_own, start_col, tile_cols, 1)
        result = jnp.zeros((NT * tile_rows, NT * tile_cols), jnp.float32)
        result = result.at[:tile_rows, :tile_cols].set(first_corner)
        result = result.at[tile_rows:, :tile_cols].set(first_cols)
        result = result.at[tile_rows : 2 * tile_rows, tile_cols : 2 * tile_cols].set(second_tile)
        result = result.at[2 * tile_rows :, tile_cols : 2 * tile_cols].set(second_cols)
        result = result.at[2 * tile_rows :, 2 * tile_cols :].set(trailing)
        result = result.reshape(NT, tile_rows, NT, tile_cols).transpose(0, 2, 1, 3)
    return result.reshape(NT, 1, NT, 1, tile_rows * tile_cols)


def solution(mesh):
    placed = (P(None, "row", None, "col", None),)
    return jax.shard_map(
        per_device,
        mesh=mesh,
        in_specs=placed,
        out_specs=P(None, "row", None, "col", None),
        check_vma=False,
    )
```

```python
import jax
import jax.numpy as jnp
from jax import lax
from jax.experimental import pallas as pl
from jax.experimental.pallas import tpu as pltpu
from jax.sharding import PartitionSpec as P

P_SIZE = 512
NT = 16


def bf16_gram(left_side, right_side):
    return lax.dot_general(
        left_side.astype(jnp.bfloat16),
        right_side.astype(jnp.bfloat16),
        (((1,), (1,)), ((), ())),
        preferred_element_type=jnp.float32,
    )


BLOCK = 128
GROUP = 4
EXACT = lax.Precision.HIGHEST


def exact_dot(left_side, right_side):
    return lax.dot_general(
        left_side, right_side, (((1,), (1,)), ((), ())),
        precision=EXACT, preferred_element_type=jnp.float32,
    )


def factor_kernel(sym_ref, low_ref, inv_ref, work_ref, diag_ref, dinv_ref):
    size = sym_ref.shape[0]
    blocks = size // BLOCK
    work_ref[...] = sym_ref[...]
    low_ref[...] = jnp.zeros_like(low_ref)
    inv_ref[...] = jnp.zeros_like(inv_ref)
    rows = lax.broadcasted_iota(jnp.int32, (BLOCK, BLOCK), 0)
    lanes = lax.broadcasted_iota(jnp.int32, (BLOCK, BLOCK), 1)
    col_ids = lax.broadcasted_iota(jnp.int32, (BLOCK, 1), 0)
    row_ids = lax.broadcasted_iota(jnp.int32, (1, BLOCK), 1)
    eye = jnp.where(rows == lanes, 1.0, 0.0).astype(jnp.float32)
    for k in range(blocks):
        here = pl.ds(k * BLOCK, BLOCK)
        diag_ref[...] = jnp.zeros((BLOCK, BLOCK), jnp.float32)
        dinv_ref[...] = eye

        def pick_col(block, at):
            return jnp.sum(jnp.where(lanes == at, block, 0.0), axis=1, keepdims=True)

        def pick_row(block, at):
            return jnp.sum(jnp.where(rows == at, block, 0.0), axis=0, keepdims=True)

        def entry(vector, at):
            return jnp.sum(jnp.where(col_ids == at, vector, 0.0), axis=0, keepdims=True)

        group = GROUP

        def step(part, block):
            base = group * part
            c_cols = []
            c_rows = []
            scales = []
            raw_cols = []
            for g in range(group):
                at = base + g
                v_col = pick_col(block, at)
                v_row = pick_row(block, at)
                for i in range(g):
                    weight = entry(raw_cols[i], at) * scales[i]
                    v_col = v_col - c_cols[i] * weight
                    v_row = v_row - c_rows[i] * weight
                root = jnp.sqrt(entry(v_col, at))
                scale = 1.0 / root
                c_cols.append(jnp.where(col_ids > at, v_col * scale, jnp.where(col_ids == at, root, 0.0)))
                c_rows.append(jnp.where(row_ids > at, v_row * scale, jnp.where(row_ids == at, root, 0.0)))
                scales.append(scale)
                raw_cols.append(v_col)
            low = diag_ref[...]
            inverse = dinv_ref[...]
            for g in range(group):
                at = base + g
                low = jnp.where(lanes == at, c_cols[g], low)
                shift = c_cols[g] * scales[g] - jnp.where(col_ids == at, scales[g], 0.0)
                inverse = inverse - shift * pick_row(inverse, at)
                block = block - c_cols[g] * c_rows[g]
            diag_ref[...] = low
            dinv_ref[...] = inverse
            return block

        lax.fori_loop(0, BLOCK // group, step, work_ref[here, here], unroll=1)
        low_ref[here, here] = diag_ref[...]
        inv_ref[here, here] = dinv_ref[...]
        if k + 1 < blocks:
            rest = pl.ds((k + 1) * BLOCK, size - (k + 1) * BLOCK)
            panel = exact_dot(work_ref[rest, here], dinv_ref[...])
            low_ref[rest, here] = panel
            work_ref[rest, rest] = work_ref[rest, rest] - exact_dot(panel, panel)
    for i in range(1, blocks):
        at_i = pl.ds(i * BLOCK, BLOCK)
        for k in range(i):
            at_k = pl.ds(k * BLOCK, BLOCK)
            total = jnp.zeros((BLOCK, BLOCK), jnp.float32)
            for m in range(k, i):
                at_m = pl.ds(m * BLOCK, BLOCK)
                total = total + jnp.dot(
                    low_ref[at_i, at_m], inv_ref[at_m, at_k],
                    precision=EXACT, preferred_element_type=jnp.float32,
                )
            inv_ref[at_i, at_k] = -jnp.dot(
                inv_ref[at_i, at_i], total,
                precision=EXACT, preferred_element_type=jnp.float32,
            )


def factor_and_inverse(sym):
    size = sym.shape[0]
    return pl.pallas_call(
        factor_kernel,
        out_shape=(
            jax.ShapeDtypeStruct((size, size), jnp.float32),
            jax.ShapeDtypeStruct((size, size), jnp.float32),
        ),
        in_specs=[pl.BlockSpec(memory_space=pltpu.VMEM)],
        out_specs=(
            pl.BlockSpec(memory_space=pltpu.VMEM),
            pl.BlockSpec(memory_space=pltpu.VMEM),
        ),
        scratch_shapes=[
            pltpu.VMEM((size, size), jnp.float32),
            pltpu.VMEM((BLOCK, BLOCK), jnp.float32),
            pltpu.VMEM((BLOCK, BLOCK), jnp.float32),
        ],
    )(sym)


def per_device(kernel):
    row_count = lax.axis_size("row")
    col_count = lax.axis_size("col")
    tile_rows = P_SIZE // row_count
    tile_cols = P_SIZE // col_count
    row_index = lax.axis_index("row")
    column_index = lax.axis_index("col")
    tiles = kernel.reshape(NT, NT, tile_rows, tile_cols)
    local = tiles.transpose(0, 2, 1, 3).reshape(NT * tile_rows, NT * tile_cols)

    with jax.named_scope("gather_inputs"):
        band = lax.all_gather(local[:, : 2 * tile_cols], "col", axis=0)
        band = band.reshape(col_count, NT * tile_rows, 2, tile_cols)
        band = band.transpose(1, 2, 0, 3).reshape(NT * tile_rows, 2 * P_SIZE)
        own_rows = band[tile_rows:].astype(jnp.float32)
        corner = lax.all_gather(band[:tile_rows, :P_SIZE], "row", axis=0, tiled=True)
        corner = corner.astype(jnp.float32)
        top = jnp.concatenate([band[: 2 * tile_rows], local[: 2 * tile_rows, 2 * tile_cols :]], axis=1)
        top = lax.all_gather(top, "row", axis=0)
        top = top.reshape(row_count, 2, tile_rows, top.shape[-1]).transpose(1, 0, 2, 3)
        top = top.reshape(2 * P_SIZE, top.shape[-1]).astype(jnp.float32)
        corners = jnp.stack([top[P_SIZE:, :P_SIZE], top[P_SIZE : 2 * P_SIZE, P_SIZE : 2 * P_SIZE]])
        own_second = lax.dynamic_slice_in_dim(top, P_SIZE + column_index * tile_cols, tile_cols, 1)
        col_rows = jnp.concatenate([own_second, top[:, 2 * P_SIZE :]], axis=1).T

    with jax.named_scope("first_panel"):
        first_factor, first_inverse = factor_and_inverse(0.5 * (corner + corner.T))
        own_count = (NT - 1) * tile_rows
        col_total = (NT - 1) * tile_cols
        stacked = jnp.concatenate(
            [corners[0], own_rows[:, :P_SIZE], col_rows[:, :P_SIZE]], axis=0
        )
        solved = exact_dot(stacked, first_inverse)
        next_rows = solved[:P_SIZE].astype(jnp.bfloat16)
        first_own = solved[P_SIZE : P_SIZE + own_count]
        first_col = solved[P_SIZE + own_count :]

    with jax.named_scope("second_panel"):
        second_corner = corners[1] - bf16_gram(next_rows, next_rows)
        second_factor, second_inverse = factor_and_inverse(0.5 * (second_corner + second_corner.T))
        own_below = own_rows[tile_rows:, P_SIZE:] - bf16_gram(first_own[tile_rows:], next_rows)
        col_below = col_rows[tile_cols:, P_SIZE:] - bf16_gram(first_col[tile_cols:], next_rows)
        solved = exact_dot(jnp.concatenate([own_below, col_below], axis=0), second_inverse)
        second_own = solved[: own_count - tile_rows]
        second_col = solved[own_count - tile_rows :]

    with jax.named_scope("trailing_update"):
        trailing = local[2 * tile_rows :, 2 * tile_cols :]
        trailing = trailing.astype(jnp.float32) - bf16_gram(
            first_own[tile_rows:], first_col[tile_cols:]
        )
        trailing = trailing - bf16_gram(second_own, second_col)

    with jax.named_scope("assemble"):
        start_row = row_index * tile_rows
        start_col = column_index * tile_cols
        first_corner = lax.dynamic_slice(first_factor, (start_row, start_col), (tile_rows, tile_cols))
        second_tile = lax.dynamic_slice(second_factor, (start_row, start_col), (tile_rows, tile_cols))
        first_cols = lax.dynamic_slice_in_dim(first_own, start_col, tile_cols, 1)
        second_cols = lax.dynamic_slice_in_dim(second_own, start_col, tile_cols, 1)
        result = jnp.zeros((NT * tile_rows, NT * tile_cols), jnp.float32)
        result = result.at[:tile_rows, :tile_cols].set(first_corner)
        result = result.at[tile_rows:, :tile_cols].set(first_cols)
        result = result.at[tile_rows : 2 * tile_rows, tile_cols : 2 * tile_cols].set(second_tile)
        result = result.at[2 * tile_rows :, tile_cols : 2 * tile_cols].set(second_cols)
        result = result.at[2 * tile_rows :, 2 * tile_cols :].set(trailing)
        result = result.reshape(NT, tile_rows, NT, tile_cols).transpose(0, 2, 1, 3)
    return result.reshape(NT, 1, NT, 1, tile_rows * tile_cols)


def solution(mesh):
    placed = (P(None, "row", None, "col", None),)
    return jax.shard_map(
        per_device,
        mesh=mesh,
        in_specs=placed,
        out_specs=P(None, "row", None, "col", None),
        check_vma=False,
    )
```

```python
import jax
import jax.numpy as jnp
from jax import lax
from jax.experimental import pallas as pl
from jax.experimental.pallas import tpu as pltpu
from jax.sharding import PartitionSpec as P

P_SIZE = 512
NT = 16


def bf16_gram(left_side, right_side):
    return lax.dot_general(
        left_side.astype(jnp.bfloat16),
        right_side.astype(jnp.bfloat16),
        (((1,), (1,)), ((), ())),
        preferred_element_type=jnp.float32,
    )


BLOCK = 128
GROUP = 4
EXACT = lax.Precision.HIGHEST


def exact_dot(left_side, right_side):
    return lax.dot_general(
        left_side, right_side, (((1,), (1,)), ((), ())),
        precision=EXACT, preferred_element_type=jnp.float32,
    )


def factor_kernel(sym_ref, low_ref, inv_ref, work_ref, diag_ref, dinv_ref):
    size = sym_ref.shape[0]
    blocks = size // BLOCK
    work_ref[...] = sym_ref[...]
    low_ref[...] = jnp.zeros_like(low_ref)
    inv_ref[...] = jnp.zeros_like(inv_ref)
    rows = lax.broadcasted_iota(jnp.int32, (BLOCK, BLOCK), 0)
    lanes = lax.broadcasted_iota(jnp.int32, (BLOCK, BLOCK), 1)
    col_ids = lax.broadcasted_iota(jnp.int32, (BLOCK, 1), 0)
    row_ids = lax.broadcasted_iota(jnp.int32, (1, BLOCK), 1)
    eye = jnp.where(rows == lanes, 1.0, 0.0).astype(jnp.float32)
    for k in range(blocks):
        here = pl.ds(k * BLOCK, BLOCK)
        diag_ref[...] = jnp.zeros((BLOCK, BLOCK), jnp.float32)
        dinv_ref[...] = eye

        def pick_col(block, at):
            return jnp.sum(jnp.where(lanes == at, block, 0.0), axis=1, keepdims=True)

        def pick_row(block, at):
            return jnp.sum(jnp.where(rows == at, block, 0.0), axis=0, keepdims=True)

        def entry(vector, at):
            return jnp.sum(jnp.where(col_ids == at, vector, 0.0), axis=0, keepdims=True)

        group = GROUP

        def step(part, block):
            base = group * part
            c_cols = []
            c_rows = []
            scales = []
            raw_cols = []
            for g in range(group):
                at = base + g
                v_col = pick_col(block, at)
                v_row = pick_row(block, at)
                for i in range(g):
                    weight = entry(raw_cols[i], at) * scales[i]
                    v_col = v_col - c_cols[i] * weight
                    v_row = v_row - c_rows[i] * weight
                root = jnp.sqrt(entry(v_col, at))
                scale = 1.0 / root
                c_cols.append(jnp.where(col_ids > at, v_col * scale, jnp.where(col_ids == at, root, 0.0)))
                c_rows.append(jnp.where(row_ids > at, v_row * scale, jnp.where(row_ids == at, root, 0.0)))
                scales.append(scale)
                raw_cols.append(v_col)
            low = diag_ref[...]
            inverse = dinv_ref[...]
            for g in range(group):
                at = base + g
                low = jnp.where(lanes == at, c_cols[g], low)
                shift = c_cols[g] * scales[g] - jnp.where(col_ids == at, scales[g], 0.0)
                inverse = inverse - shift * pick_row(inverse, at)
                block = block - c_cols[g] * c_rows[g]
            diag_ref[...] = low
            dinv_ref[...] = inverse
            return block

        lax.fori_loop(0, BLOCK // group, step, work_ref[here, here], unroll=1)
        low_ref[here, here] = diag_ref[...]
        inv_ref[here, here] = dinv_ref[...]
        if k + 1 < blocks:
            rest = pl.ds((k + 1) * BLOCK, size - (k + 1) * BLOCK)
            panel = exact_dot(work_ref[rest, here], dinv_ref[...])
            low_ref[rest, here] = panel
            work_ref[rest, rest] = work_ref[rest, rest] - exact_dot(panel, panel)
    for i in range(1, blocks):
        at_i = pl.ds(i * BLOCK, BLOCK)
        for k in range(i):
            at_k = pl.ds(k * BLOCK, BLOCK)
            total = jnp.zeros((BLOCK, BLOCK), jnp.float32)
            for m in range(k, i):
                at_m = pl.ds(m * BLOCK, BLOCK)
                total = total + jnp.dot(
                    low_ref[at_i, at_m], inv_ref[at_m, at_k],
                    precision=EXACT, preferred_element_type=jnp.float32,
                )
            inv_ref[at_i, at_k] = -jnp.dot(
                inv_ref[at_i, at_i], total,
                precision=EXACT, preferred_element_type=jnp.float32,
            )


def factor_and_inverse(sym):
    size = sym.shape[0]
    return pl.pallas_call(
        factor_kernel,
        out_shape=(
            jax.ShapeDtypeStruct((size, size), jnp.float32),
            jax.ShapeDtypeStruct((size, size), jnp.float32),
        ),
        in_specs=[pl.BlockSpec(memory_space=pltpu.VMEM)],
        out_specs=(
            pl.BlockSpec(memory_space=pltpu.VMEM),
            pl.BlockSpec(memory_space=pltpu.VMEM),
        ),
        scratch_shapes=[
            pltpu.VMEM((size, size), jnp.float32),
            pltpu.VMEM((BLOCK, BLOCK), jnp.float32),
            pltpu.VMEM((BLOCK, BLOCK), jnp.float32),
        ],
    )(sym)


def per_device(kernel):
    row_count = lax.axis_size("row")
    col_count = lax.axis_size("col")
    tile_rows = P_SIZE // row_count
    tile_cols = P_SIZE // col_count
    row_index = lax.axis_index("row")
    column_index = lax.axis_index("col")
    tiles = kernel.reshape(NT, NT, tile_rows, tile_cols)
    local = tiles.transpose(0, 2, 1, 3).reshape(NT * tile_rows, NT * tile_cols)

    with jax.named_scope("gather_inputs"):
        band = lax.all_gather(local[:, : 2 * tile_cols], "col", axis=0)
        band = band.reshape(col_count, NT * tile_rows, 2, tile_cols)
        band = band.transpose(1, 2, 0, 3).reshape(NT * tile_rows, 2 * P_SIZE)
        own_rows = band[tile_rows:].astype(jnp.float32)
        corner = lax.all_gather(band[:tile_rows, :P_SIZE], "row", axis=0, tiled=True)
        corner = corner.astype(jnp.float32)
        top = jnp.concatenate([band[: 2 * tile_rows], local[: 2 * tile_rows, 2 * tile_cols :]], axis=1)
        top = lax.all_gather(top, "row", axis=0)
        top = top.reshape(row_count, 2, tile_rows, top.shape[-1]).transpose(1, 0, 2, 3)
        top = top.reshape(2 * P_SIZE, top.shape[-1]).astype(jnp.float32)
        corners = jnp.stack([top[P_SIZE:, :P_SIZE], top[P_SIZE : 2 * P_SIZE, P_SIZE : 2 * P_SIZE]])
        own_second = lax.dynamic_slice_in_dim(top, P_SIZE + column_index * tile_cols, tile_cols, 1)
        col_rows = jnp.concatenate([own_second, top[:, 2 * P_SIZE :]], axis=1).T

    with jax.named_scope("first_panel"):
        first_factor, first_inverse = factor_and_inverse(0.5 * (corner + corner.T))
        own_count = (NT - 1) * tile_rows
        col_total = (NT - 1) * tile_cols
        stacked = jnp.concatenate(
            [corners[0], own_rows[:, :P_SIZE], col_rows[:, :P_SIZE]], axis=0
        )
        solved = exact_dot(stacked, first_inverse)
        next_rows = solved[:P_SIZE].astype(jnp.bfloat16)
        first_own = solved[P_SIZE : P_SIZE + own_count]
        first_col = solved[P_SIZE + own_count :]

    with jax.named_scope("second_panel"):
        second_corner = corners[1] - bf16_gram(next_rows, next_rows)
        second_factor, second_inverse = factor_and_inverse(0.5 * (second_corner + second_corner.T))
        own_below = own_rows[tile_rows:, P_SIZE:] - bf16_gram(first_own[tile_rows:], next_rows)
        col_below = col_rows[tile_cols:, P_SIZE:] - bf16_gram(first_col[tile_cols:], next_rows)
        solved = exact_dot(jnp.concatenate([own_below, col_below], axis=0), second_inverse)
        second_own = solved[: own_count - tile_rows]
        second_col = solved[own_count - tile_rows :]

    with jax.named_scope("trailing_update"):
        trailing = local[2 * tile_rows :, 2 * tile_cols :]
        trailing = trailing.astype(jnp.float32) - bf16_gram(
            first_own[tile_rows:], first_col[tile_cols:]
        )
        trailing = trailing - bf16_gram(second_own, second_col)

    with jax.named_scope("assemble"):
        start_row = row_index * tile_rows
        start_col = column_index * tile_cols
        first_corner = lax.dynamic_slice(first_factor, (start_row, start_col), (tile_rows, tile_cols))
        second_tile = lax.dynamic_slice(second_factor, (start_row, start_col), (tile_rows, tile_cols))
        first_cols = lax.dynamic_slice_in_dim(first_own, start_col, tile_cols, 1)
        second_cols = lax.dynamic_slice_in_dim(second_own, start_col, tile_cols, 1)
        width = NT * tile_cols
        first_block = jnp.concatenate(
            [first_corner, jnp.zeros((tile_rows, width - tile_cols), jnp.float32)], axis=1
        )
        second_block = jnp.concatenate(
            [
                first_cols[:tile_rows],
                second_tile,
                jnp.zeros((tile_rows, width - 2 * tile_cols), jnp.float32),
            ],
            axis=1,
        )
        rest_block = jnp.concatenate([first_cols[tile_rows:], second_cols, trailing], axis=1)
        result = jnp.concatenate([first_block, second_block, rest_block], axis=0)
        result = result.reshape(NT, tile_rows, NT, tile_cols).transpose(0, 2, 1, 3)
    return result.reshape(NT, 1, NT, 1, tile_rows * tile_cols)


def solution(mesh):
    placed = (P(None, "row", None, "col", None),)
    return jax.shard_map(
        per_device,
        mesh=mesh,
        in_specs=placed,
        out_specs=P(None, "row", None, "col", None),
        check_vma=False,
    )
```

```python
import jax
import jax.numpy as jnp
from jax import lax
from jax.experimental import pallas as pl
from jax.experimental.pallas import tpu as pltpu
from jax.sharding import PartitionSpec as P

P_SIZE = 512
NT = 16


def bf16_gram(left_side, right_side):
    return lax.dot_general(
        left_side.astype(jnp.bfloat16),
        right_side.astype(jnp.bfloat16),
        (((1,), (1,)), ((), ())),
        preferred_element_type=jnp.float32,
    )


BLOCK = 128
GROUP = 4
EXACT = lax.Precision.HIGHEST


def exact_dot(left_side, right_side):
    return lax.dot_general(
        left_side, right_side, (((1,), (1,)), ((), ())),
        precision=EXACT, preferred_element_type=jnp.float32,
    )


def column_dot(columns, right_side):
    return lax.dot_general(
        columns, right_side, (((0,), (1,)), ((), ())),
        precision=EXACT, preferred_element_type=jnp.float32,
    )


def factor_kernel(sym_ref, low_ref, inv_ref, work_ref, diag_ref, dinv_ref):
    size = sym_ref.shape[0]
    blocks = size // BLOCK
    work_ref[...] = sym_ref[...]
    low_ref[...] = jnp.zeros_like(low_ref)
    inv_ref[...] = jnp.zeros_like(inv_ref)
    rows = lax.broadcasted_iota(jnp.int32, (BLOCK, BLOCK), 0)
    lanes = lax.broadcasted_iota(jnp.int32, (BLOCK, BLOCK), 1)
    col_ids = lax.broadcasted_iota(jnp.int32, (BLOCK, 1), 0)
    row_ids = lax.broadcasted_iota(jnp.int32, (1, BLOCK), 1)
    eye = jnp.where(rows == lanes, 1.0, 0.0).astype(jnp.float32)
    for k in range(blocks):
        here = pl.ds(k * BLOCK, BLOCK)
        diag_ref[...] = jnp.zeros((BLOCK, BLOCK), jnp.float32)
        dinv_ref[...] = eye

        def pick_col(block, at):
            return jnp.sum(jnp.where(lanes == at, block, 0.0), axis=1, keepdims=True)

        def pick_row(block, at):
            return jnp.sum(jnp.where(rows == at, block, 0.0), axis=0, keepdims=True)

        def entry(vector, at):
            return jnp.sum(jnp.where(col_ids == at, vector, 0.0), axis=0, keepdims=True)

        group = GROUP

        def step(part, block):
            base = group * part
            c_cols = []
            c_rows = []
            scales = []
            raw_cols = []
            for g in range(group):
                at = base + g
                v_col = pick_col(block, at)
                v_row = pick_row(block, at)
                for i in range(g):
                    weight = entry(raw_cols[i], at) * scales[i]
                    v_col = v_col - c_cols[i] * weight
                    v_row = v_row - c_rows[i] * weight
                root = jnp.sqrt(entry(v_col, at))
                scale = 1.0 / root
                c_cols.append(jnp.where(col_ids > at, v_col * scale, jnp.where(col_ids == at, root, 0.0)))
                c_rows.append(jnp.where(row_ids > at, v_row * scale, jnp.where(row_ids == at, root, 0.0)))
                scales.append(scale)
                raw_cols.append(v_col)
            low = diag_ref[...]
            inverse = dinv_ref[...]
            for g in range(group):
                at = base + g
                low = jnp.where(lanes == at, c_cols[g], low)
                shift = c_cols[g] * scales[g] - jnp.where(col_ids == at, scales[g], 0.0)
                inverse = inverse - shift * pick_row(inverse, at)
                block = block - c_cols[g] * c_rows[g]
            diag_ref[...] = low
            dinv_ref[...] = inverse
            return block

        lax.fori_loop(0, BLOCK // group, step, work_ref[here, here], unroll=1)
        low_ref[here, here] = diag_ref[...]
        inv_ref[here, here] = dinv_ref[...]
        if k + 1 < blocks:
            rest = pl.ds((k + 1) * BLOCK, size - (k + 1) * BLOCK)
            panel = exact_dot(work_ref[rest, here], dinv_ref[...])
            low_ref[rest, here] = panel
            work_ref[rest, rest] = work_ref[rest, rest] - exact_dot(panel, panel)
    for i in range(1, blocks):
        at_i = pl.ds(i * BLOCK, BLOCK)
        for k in range(i):
            at_k = pl.ds(k * BLOCK, BLOCK)
            total = jnp.zeros((BLOCK, BLOCK), jnp.float32)
            for m in range(k, i):
                at_m = pl.ds(m * BLOCK, BLOCK)
                total = total + jnp.dot(
                    low_ref[at_i, at_m], inv_ref[at_m, at_k],
                    precision=EXACT, preferred_element_type=jnp.float32,
                )
            inv_ref[at_i, at_k] = -jnp.dot(
                inv_ref[at_i, at_i], total,
                precision=EXACT, preferred_element_type=jnp.float32,
            )


def factor_and_inverse(sym):
    size = sym.shape[0]
    return pl.pallas_call(
        factor_kernel,
        out_shape=(
            jax.ShapeDtypeStruct((size, size), jnp.float32),
            jax.ShapeDtypeStruct((size, size), jnp.float32),
        ),
        in_specs=[pl.BlockSpec(memory_space=pltpu.VMEM)],
        out_specs=(
            pl.BlockSpec(memory_space=pltpu.VMEM),
            pl.BlockSpec(memory_space=pltpu.VMEM),
        ),
        scratch_shapes=[
            pltpu.VMEM((size, size), jnp.float32),
            pltpu.VMEM((BLOCK, BLOCK), jnp.float32),
            pltpu.VMEM((BLOCK, BLOCK), jnp.float32),
        ],
    )(sym)


def per_device(kernel):
    row_count = lax.axis_size("row")
    col_count = lax.axis_size("col")
    tile_rows = P_SIZE // row_count
    tile_cols = P_SIZE // col_count
    row_index = lax.axis_index("row")
    column_index = lax.axis_index("col")
    tiles = kernel.reshape(NT, NT, tile_rows, tile_cols)
    local = tiles.transpose(0, 2, 1, 3).reshape(NT * tile_rows, NT * tile_cols)

    with jax.named_scope("gather_inputs"):
        band = lax.all_gather(local[:, : 2 * tile_cols], "col", axis=0)
        band = band.reshape(col_count, NT * tile_rows, 2, tile_cols)
        band = band.transpose(1, 2, 0, 3).reshape(NT * tile_rows, 2 * P_SIZE)
        own_rows = band[tile_rows:].astype(jnp.float32)
        corner = lax.all_gather(band[:tile_rows, :P_SIZE], "row", axis=0, tiled=True)
        corner = corner.astype(jnp.float32)
        top = jnp.concatenate([band[: 2 * tile_rows], local[: 2 * tile_rows, 2 * tile_cols :]], axis=1)
        top = lax.all_gather(top, "row", axis=0)
        top = top.reshape(row_count, 2, tile_rows, top.shape[-1]).transpose(1, 0, 2, 3)
        top = top.reshape(2 * P_SIZE, top.shape[-1])
        corners = jnp.stack([top[P_SIZE:, :P_SIZE], top[P_SIZE : 2 * P_SIZE, P_SIZE : 2 * P_SIZE]])
        corners = corners.astype(jnp.float32)
        own_second = lax.dynamic_slice_in_dim(top, P_SIZE + column_index * tile_cols, tile_cols, 1)
        col_cols = jnp.concatenate([own_second, top[:, 2 * P_SIZE :]], axis=1).astype(jnp.float32)

    with jax.named_scope("first_panel"):
        first_factor, first_inverse = factor_and_inverse(0.5 * (corner + corner.T))
        own_count = (NT - 1) * tile_rows
        stacked = jnp.concatenate([corners[0], own_rows[:, :P_SIZE]], axis=0)
        solved = exact_dot(stacked, first_inverse)
        next_rows = solved[:P_SIZE].astype(jnp.bfloat16)
        first_own = solved[P_SIZE:]
        first_col = column_dot(col_cols[:P_SIZE], first_inverse)

    with jax.named_scope("second_panel"):
        second_corner = corners[1] - bf16_gram(next_rows, next_rows)
        second_factor, second_inverse = factor_and_inverse(0.5 * (second_corner + second_corner.T))
        own_below = own_rows[tile_rows:, P_SIZE:] - bf16_gram(first_own[tile_rows:], next_rows)
        col_below = col_cols[P_SIZE:, tile_cols:] - bf16_gram(next_rows, first_col[tile_cols:])
        second_own = exact_dot(own_below, second_inverse)
        second_col = column_dot(col_below, second_inverse)

    with jax.named_scope("trailing_update"):
        trailing = local[2 * tile_rows :, 2 * tile_cols :]
        trailing = trailing.astype(jnp.float32) - bf16_gram(
            first_own[tile_rows:], first_col[tile_cols:]
        )
        trailing = trailing - bf16_gram(second_own, second_col)

    with jax.named_scope("assemble"):
        start_row = row_index * tile_rows
        start_col = column_index * tile_cols
        first_corner = lax.dynamic_slice(first_factor, (start_row, start_col), (tile_rows, tile_cols))
        second_tile = lax.dynamic_slice(second_factor, (start_row, start_col), (tile_rows, tile_cols))
        first_cols = lax.dynamic_slice_in_dim(first_own, start_col, tile_cols, 1)
        second_cols = lax.dynamic_slice_in_dim(second_own, start_col, tile_cols, 1)
        width = NT * tile_cols
        first_block = jnp.concatenate(
            [first_corner, jnp.zeros((tile_rows, width - tile_cols), jnp.float32)], axis=1
        )
        second_block = jnp.concatenate(
            [
                first_cols[:tile_rows],
                second_tile,
                jnp.zeros((tile_rows, width - 2 * tile_cols), jnp.float32),
            ],
            axis=1,
        )
        rest_block = jnp.concatenate([first_cols[tile_rows:], second_cols, trailing], axis=1)
        result = jnp.concatenate([first_block, second_block, rest_block], axis=0)
        result = result.reshape(NT, tile_rows, NT, tile_cols).transpose(0, 2, 1, 3)
    return result.reshape(NT, 1, NT, 1, tile_rows * tile_cols)


def solution(mesh):
    placed = (P(None, "row", None, "col", None),)
    return jax.shard_map(
        per_device,
        mesh=mesh,
        in_specs=placed,
        out_specs=P(None, "row", None, "col", None),
        check_vma=False,
    )
```

```python
import jax
import jax.numpy as jnp
from jax import lax
from jax.experimental import pallas as pl
from jax.experimental.pallas import tpu as pltpu
from jax.sharding import PartitionSpec as P

P_SIZE = 512
NT = 16


def bf16_gram(left_side, right_side):
    return lax.dot_general(
        left_side.astype(jnp.bfloat16),
        right_side.astype(jnp.bfloat16),
        (((1,), (1,)), ((), ())),
        preferred_element_type=jnp.float32,
    )


BLOCK = 128
GROUP = 4
EXACT = lax.Precision.HIGHEST


def exact_dot(left_side, right_side):
    return lax.dot_general(
        left_side, right_side, (((1,), (1,)), ((), ())),
        precision=EXACT, preferred_element_type=jnp.float32,
    )


def solve_dot(left_side, right_side):
    return lax.dot_general(
        left_side, right_side, (((1,), (1,)), ((), ())),
        precision=lax.Precision.HIGH, preferred_element_type=jnp.float32,
    )


def factor_kernel(sym_ref, low_ref, inv_ref, work_ref, diag_ref, dinv_ref):
    size = sym_ref.shape[0]
    blocks = size // BLOCK
    work_ref[...] = sym_ref[...]
    low_ref[...] = jnp.zeros_like(low_ref)
    inv_ref[...] = jnp.zeros_like(inv_ref)
    rows = lax.broadcasted_iota(jnp.int32, (BLOCK, BLOCK), 0)
    lanes = lax.broadcasted_iota(jnp.int32, (BLOCK, BLOCK), 1)
    col_ids = lax.broadcasted_iota(jnp.int32, (BLOCK, 1), 0)
    row_ids = lax.broadcasted_iota(jnp.int32, (1, BLOCK), 1)
    eye = jnp.where(rows == lanes, 1.0, 0.0).astype(jnp.float32)
    for k in range(blocks):
        here = pl.ds(k * BLOCK, BLOCK)
        diag_ref[...] = jnp.zeros((BLOCK, BLOCK), jnp.float32)
        dinv_ref[...] = eye

        def pick_col(block, at):
            return jnp.sum(jnp.where(lanes == at, block, 0.0), axis=1, keepdims=True)

        def pick_row(block, at):
            return jnp.sum(jnp.where(rows == at, block, 0.0), axis=0, keepdims=True)

        def entry(vector, at):
            return jnp.sum(jnp.where(col_ids == at, vector, 0.0), axis=0, keepdims=True)

        group = GROUP

        def step(part, block):
            base = group * part
            c_cols = []
            c_rows = []
            scales = []
            raw_cols = []
            for g in range(group):
                at = base + g
                v_col = pick_col(block, at)
                v_row = pick_row(block, at)
                for i in range(g):
                    weight = entry(raw_cols[i], at) * scales[i]
                    v_col = v_col - c_cols[i] * weight
                    v_row = v_row - c_rows[i] * weight
                root = jnp.sqrt(entry(v_col, at))
                scale = 1.0 / root
                c_cols.append(jnp.where(col_ids > at, v_col * scale, jnp.where(col_ids == at, root, 0.0)))
                c_rows.append(jnp.where(row_ids > at, v_row * scale, jnp.where(row_ids == at, root, 0.0)))
                scales.append(scale)
                raw_cols.append(v_col)
            low = diag_ref[...]
            inverse = dinv_ref[...]
            for g in range(group):
                at = base + g
                low = jnp.where(lanes == at, c_cols[g], low)
                shift = c_cols[g] * scales[g] - jnp.where(col_ids == at, scales[g], 0.0)
                inverse = inverse - shift * pick_row(inverse, at)
                block = block - c_cols[g] * c_rows[g]
            diag_ref[...] = low
            dinv_ref[...] = inverse
            return block

        lax.fori_loop(0, BLOCK // group, step, work_ref[here, here], unroll=1)
        low_ref[here, here] = diag_ref[...]
        inv_ref[here, here] = dinv_ref[...]
        if k + 1 < blocks:
            rest = pl.ds((k + 1) * BLOCK, size - (k + 1) * BLOCK)
            panel = exact_dot(work_ref[rest, here], dinv_ref[...])
            low_ref[rest, here] = panel
            work_ref[rest, rest] = work_ref[rest, rest] - exact_dot(panel, panel)
    for i in range(1, blocks):
        at_i = pl.ds(i * BLOCK, BLOCK)
        for k in range(i):
            at_k = pl.ds(k * BLOCK, BLOCK)
            total = jnp.zeros((BLOCK, BLOCK), jnp.float32)
            for m in range(k, i):
                at_m = pl.ds(m * BLOCK, BLOCK)
                total = total + jnp.dot(
                    low_ref[at_i, at_m], inv_ref[at_m, at_k],
                    precision=EXACT, preferred_element_type=jnp.float32,
                )
            inv_ref[at_i, at_k] = -jnp.dot(
                inv_ref[at_i, at_i], total,
                precision=EXACT, preferred_element_type=jnp.float32,
            )


def factor_and_inverse(sym):
    size = sym.shape[0]
    return pl.pallas_call(
        factor_kernel,
        out_shape=(
            jax.ShapeDtypeStruct((size, size), jnp.float32),
            jax.ShapeDtypeStruct((size, size), jnp.float32),
        ),
        in_specs=[pl.BlockSpec(memory_space=pltpu.VMEM)],
        out_specs=(
            pl.BlockSpec(memory_space=pltpu.VMEM),
            pl.BlockSpec(memory_space=pltpu.VMEM),
        ),
        scratch_shapes=[
            pltpu.VMEM((size, size), jnp.float32),
            pltpu.VMEM((BLOCK, BLOCK), jnp.float32),
            pltpu.VMEM((BLOCK, BLOCK), jnp.float32),
        ],
    )(sym)


def per_device(kernel):
    row_count = lax.axis_size("row")
    col_count = lax.axis_size("col")
    tile_rows = P_SIZE // row_count
    tile_cols = P_SIZE // col_count
    row_index = lax.axis_index("row")
    column_index = lax.axis_index("col")
    tiles = kernel.reshape(NT, NT, tile_rows, tile_cols)
    local = tiles.transpose(0, 2, 1, 3).reshape(NT * tile_rows, NT * tile_cols)

    with jax.named_scope("gather_inputs"):
        band = lax.all_gather(local[:, : 2 * tile_cols], "col", axis=0)
        band = band.reshape(col_count, NT * tile_rows, 2, tile_cols)
        band = band.transpose(1, 2, 0, 3).reshape(NT * tile_rows, 2 * P_SIZE)
        own_rows = band[tile_rows:].astype(jnp.float32)
        corner = lax.all_gather(band[:tile_rows, :P_SIZE], "row", axis=0, tiled=True)
        corner = corner.astype(jnp.float32)
        top = jnp.concatenate([band[: 2 * tile_rows], local[: 2 * tile_rows, 2 * tile_cols :]], axis=1)
        top = lax.all_gather(top, "row", axis=0)
        top = top.reshape(row_count, 2, tile_rows, top.shape[-1]).transpose(1, 0, 2, 3)
        top = top.reshape(2 * P_SIZE, top.shape[-1]).astype(jnp.float32)
        corners = jnp.stack([top[P_SIZE:, :P_SIZE], top[P_SIZE : 2 * P_SIZE, P_SIZE : 2 * P_SIZE]])
        own_second = lax.dynamic_slice_in_dim(top, P_SIZE + column_index * tile_cols, tile_cols, 1)
        col_rows = jnp.concatenate([own_second, top[:, 2 * P_SIZE :]], axis=1).T

    with jax.named_scope("first_panel"):
        first_factor, first_inverse = factor_and_inverse(0.5 * (corner + corner.T))
        own_count = (NT - 1) * tile_rows
        col_total = (NT - 1) * tile_cols
        stacked = jnp.concatenate(
            [corners[0], own_rows[:, :P_SIZE], col_rows[:, :P_SIZE]], axis=0
        )
        solved = solve_dot(stacked, first_inverse)
        next_rows = solved[:P_SIZE].astype(jnp.bfloat16)
        first_own = solved[P_SIZE : P_SIZE + own_count]
        first_col = solved[P_SIZE + own_count :]

    with jax.named_scope("second_panel"):
        second_corner = corners[1] - bf16_gram(next_rows, next_rows)
        second_factor, second_inverse = factor_and_inverse(0.5 * (second_corner + second_corner.T))
        own_below = own_rows[tile_rows:, P_SIZE:] - bf16_gram(first_own[tile_rows:], next_rows)
        col_below = col_rows[tile_cols:, P_SIZE:] - bf16_gram(first_col[tile_cols:], next_rows)
        solved = solve_dot(jnp.concatenate([own_below, col_below], axis=0), second_inverse)
        second_own = solved[: own_count - tile_rows]
        second_col = solved[own_count - tile_rows :]

    with jax.named_scope("trailing_update"):
        trailing = local[2 * tile_rows :, 2 * tile_cols :]
        trailing = trailing.astype(jnp.float32) - bf16_gram(
            first_own[tile_rows:], first_col[tile_cols:]
        )
        trailing = trailing - bf16_gram(second_own, second_col)

    with jax.named_scope("assemble"):
        start_row = row_index * tile_rows
        start_col = column_index * tile_cols
        first_corner = lax.dynamic_slice(first_factor, (start_row, start_col), (tile_rows, tile_cols))
        second_tile = lax.dynamic_slice(second_factor, (start_row, start_col), (tile_rows, tile_cols))
        first_cols = lax.dynamic_slice_in_dim(first_own, start_col, tile_cols, 1)
        second_cols = lax.dynamic_slice_in_dim(second_own, start_col, tile_cols, 1)
        width = NT * tile_cols
        first_block = jnp.concatenate(
            [first_corner, jnp.zeros((tile_rows, width - tile_cols), jnp.float32)], axis=1
        )
        second_block = jnp.concatenate(
            [
                first_cols[:tile_rows],
                second_tile,
                jnp.zeros((tile_rows, width - 2 * tile_cols), jnp.float32),
            ],
            axis=1,
        )
        rest_block = jnp.concatenate([first_cols[tile_rows:], second_cols, trailing], axis=1)
        result = jnp.concatenate([first_block, second_block, rest_block], axis=0)
        result = result.reshape(NT, tile_rows, NT, tile_cols).transpose(0, 2, 1, 3)
    return result.reshape(NT, 1, NT, 1, tile_rows * tile_cols)


def solution(mesh):
    placed = (P(None, "row", None, "col", None),)
    return jax.shard_map(
        per_device,
        mesh=mesh,
        in_specs=placed,
        out_specs=P(None, "row", None, "col", None),
        check_vma=False,
    )
```

```python
import jax
import jax.numpy as jnp
from jax import lax
from jax.experimental import pallas as pl
from jax.experimental.pallas import tpu as pltpu
from jax.sharding import PartitionSpec as P

P_SIZE = 512
NT = 16


def bf16_gram(left_side, right_side):
    return lax.dot_general(
        left_side.astype(jnp.bfloat16),
        right_side.astype(jnp.bfloat16),
        (((1,), (1,)), ((), ())),
        preferred_element_type=jnp.float32,
    )


BLOCK = 128
GROUP = 4
EXACT = lax.Precision.HIGHEST


def exact_dot(left_side, right_side):
    return lax.dot_general(
        left_side, right_side, (((1,), (1,)), ((), ())),
        precision=EXACT, preferred_element_type=jnp.float32,
    )


def split_dot(narrow_side, right_side):
    parts = []
    remainder = right_side
    for _ in range(3):
        piece = lax.reduce_precision(remainder, exponent_bits=8, mantissa_bits=7)
        parts.append(piece.astype(jnp.bfloat16))
        remainder = remainder - piece
    narrow_side = narrow_side.astype(jnp.bfloat16)
    total = bf16_gram(narrow_side, parts[0])
    return total + (bf16_gram(narrow_side, parts[1]) + bf16_gram(narrow_side, parts[2]))


def factor_kernel(sym_ref, low_ref, inv_ref, work_ref, diag_ref, dinv_ref):
    size = sym_ref.shape[0]
    blocks = size // BLOCK
    work_ref[...] = sym_ref[...]
    low_ref[...] = jnp.zeros_like(low_ref)
    inv_ref[...] = jnp.zeros_like(inv_ref)
    rows = lax.broadcasted_iota(jnp.int32, (BLOCK, BLOCK), 0)
    lanes = lax.broadcasted_iota(jnp.int32, (BLOCK, BLOCK), 1)
    col_ids = lax.broadcasted_iota(jnp.int32, (BLOCK, 1), 0)
    row_ids = lax.broadcasted_iota(jnp.int32, (1, BLOCK), 1)
    eye = jnp.where(rows == lanes, 1.0, 0.0).astype(jnp.float32)
    for k in range(blocks):
        here = pl.ds(k * BLOCK, BLOCK)
        diag_ref[...] = jnp.zeros((BLOCK, BLOCK), jnp.float32)
        dinv_ref[...] = eye

        def pick_col(block, at):
            return jnp.sum(jnp.where(lanes == at, block, 0.0), axis=1, keepdims=True)

        def pick_row(block, at):
            return jnp.sum(jnp.where(rows == at, block, 0.0), axis=0, keepdims=True)

        def entry(vector, at):
            return jnp.sum(jnp.where(col_ids == at, vector, 0.0), axis=0, keepdims=True)

        group = GROUP

        def step(part, block):
            base = group * part
            c_cols = []
            c_rows = []
            scales = []
            raw_cols = []
            for g in range(group):
                at = base + g
                v_col = pick_col(block, at)
                v_row = pick_row(block, at)
                for i in range(g):
                    weight = entry(raw_cols[i], at) * scales[i]
                    v_col = v_col - c_cols[i] * weight
                    v_row = v_row - c_rows[i] * weight
                root = jnp.sqrt(entry(v_col, at))
                scale = 1.0 / root
                c_cols.append(jnp.where(col_ids > at, v_col * scale, jnp.where(col_ids == at, root, 0.0)))
                c_rows.append(jnp.where(row_ids > at, v_row * scale, jnp.where(row_ids == at, root, 0.0)))
                scales.append(scale)
                raw_cols.append(v_col)
            low = diag_ref[...]
            inverse = dinv_ref[...]
            for g in range(group):
                at = base + g
                low = jnp.where(lanes == at, c_cols[g], low)
                shift = c_cols[g] * scales[g] - jnp.where(col_ids == at, scales[g], 0.0)
                inverse = inverse - shift * pick_row(inverse, at)
                block = block - c_cols[g] * c_rows[g]
            diag_ref[...] = low
            dinv_ref[...] = inverse
            return block

        lax.fori_loop(0, BLOCK // group, step, work_ref[here, here], unroll=1)
        low_ref[here, here] = diag_ref[...]
        inv_ref[here, here] = dinv_ref[...]
        if k + 1 < blocks:
            rest = pl.ds((k + 1) * BLOCK, size - (k + 1) * BLOCK)
            panel = exact_dot(work_ref[rest, here], dinv_ref[...])
            low_ref[rest, here] = panel
            work_ref[rest, rest] = work_ref[rest, rest] - exact_dot(panel, panel)
    for i in range(1, blocks):
        at_i = pl.ds(i * BLOCK, BLOCK)
        for k in range(i):
            at_k = pl.ds(k * BLOCK, BLOCK)
            total = jnp.zeros((BLOCK, BLOCK), jnp.float32)
            for m in range(k, i):
                at_m = pl.ds(m * BLOCK, BLOCK)
                total = total + jnp.dot(
                    low_ref[at_i, at_m], inv_ref[at_m, at_k],
                    precision=EXACT, preferred_element_type=jnp.float32,
                )
            inv_ref[at_i, at_k] = -jnp.dot(
                inv_ref[at_i, at_i], total,
                precision=EXACT, preferred_element_type=jnp.float32,
            )


def factor_and_inverse(sym):
    size = sym.shape[0]
    return pl.pallas_call(
        factor_kernel,
        out_shape=(
            jax.ShapeDtypeStruct((size, size), jnp.float32),
            jax.ShapeDtypeStruct((size, size), jnp.float32),
        ),
        in_specs=[pl.BlockSpec(memory_space=pltpu.VMEM)],
        out_specs=(
            pl.BlockSpec(memory_space=pltpu.VMEM),
            pl.BlockSpec(memory_space=pltpu.VMEM),
        ),
        scratch_shapes=[
            pltpu.VMEM((size, size), jnp.float32),
            pltpu.VMEM((BLOCK, BLOCK), jnp.float32),
            pltpu.VMEM((BLOCK, BLOCK), jnp.float32),
        ],
    )(sym)


def per_device(kernel):
    row_count = lax.axis_size("row")
    col_count = lax.axis_size("col")
    tile_rows = P_SIZE // row_count
    tile_cols = P_SIZE // col_count
    row_index = lax.axis_index("row")
    column_index = lax.axis_index("col")
    tiles = kernel.reshape(NT, NT, tile_rows, tile_cols)
    local = tiles.transpose(0, 2, 1, 3).reshape(NT * tile_rows, NT * tile_cols)

    with jax.named_scope("gather_inputs"):
        band = lax.all_gather(local[:, : 2 * tile_cols], "col", axis=0)
        band = band.reshape(col_count, NT * tile_rows, 2, tile_cols)
        band = band.transpose(1, 2, 0, 3).reshape(NT * tile_rows, 2 * P_SIZE)
        own_rows = band[tile_rows:].astype(jnp.float32)
        corner = lax.all_gather(band[:tile_rows, :P_SIZE], "row", axis=0, tiled=True)
        corner = corner.astype(jnp.float32)
        top = jnp.concatenate([band[: 2 * tile_rows], local[: 2 * tile_rows, 2 * tile_cols :]], axis=1)
        top = lax.all_gather(top, "row", axis=0)
        top = top.reshape(row_count, 2, tile_rows, top.shape[-1]).transpose(1, 0, 2, 3)
        top = top.reshape(2 * P_SIZE, top.shape[-1]).astype(jnp.float32)
        corners = jnp.stack([top[P_SIZE:, :P_SIZE], top[P_SIZE : 2 * P_SIZE, P_SIZE : 2 * P_SIZE]])
        own_second = lax.dynamic_slice_in_dim(top, P_SIZE + column_index * tile_cols, tile_cols, 1)
        col_rows = jnp.concatenate([own_second, top[:, 2 * P_SIZE :]], axis=1).T

    with jax.named_scope("first_panel"):
        first_factor, first_inverse = factor_and_inverse(0.5 * (corner + corner.T))
        own_count = (NT - 1) * tile_rows
        col_total = (NT - 1) * tile_cols
        stacked = jnp.concatenate(
            [corners[0], own_rows[:, :P_SIZE], col_rows[:, :P_SIZE]], axis=0
        )
        solved = split_dot(stacked, first_inverse)
        next_rows = solved[:P_SIZE].astype(jnp.bfloat16)
        first_own = solved[P_SIZE : P_SIZE + own_count]
        first_col = solved[P_SIZE + own_count :]

    with jax.named_scope("second_panel"):
        second_corner = corners[1] - bf16_gram(next_rows, next_rows)
        second_factor, second_inverse = factor_and_inverse(0.5 * (second_corner + second_corner.T))
        own_below = own_rows[tile_rows:, P_SIZE:] - bf16_gram(first_own[tile_rows:], next_rows)
        col_below = col_rows[tile_cols:, P_SIZE:] - bf16_gram(first_col[tile_cols:], next_rows)
        solved = exact_dot(jnp.concatenate([own_below, col_below], axis=0), second_inverse)
        second_own = solved[: own_count - tile_rows]
        second_col = solved[own_count - tile_rows :]

    with jax.named_scope("trailing_update"):
        trailing = local[2 * tile_rows :, 2 * tile_cols :]
        trailing = trailing.astype(jnp.float32) - bf16_gram(
            first_own[tile_rows:], first_col[tile_cols:]
        )
        trailing = trailing - bf16_gram(second_own, second_col)

    with jax.named_scope("assemble"):
        start_row = row_index * tile_rows
        start_col = column_index * tile_cols
        first_corner = lax.dynamic_slice(first_factor, (start_row, start_col), (tile_rows, tile_cols))
        second_tile = lax.dynamic_slice(second_factor, (start_row, start_col), (tile_rows, tile_cols))
        first_cols = lax.dynamic_slice_in_dim(first_own, start_col, tile_cols, 1)
        second_cols = lax.dynamic_slice_in_dim(second_own, start_col, tile_cols, 1)
        width = NT * tile_cols
        first_block = jnp.concatenate(
            [first_corner, jnp.zeros((tile_rows, width - tile_cols), jnp.float32)], axis=1
        )
        second_block = jnp.concatenate(
            [
                first_cols[:tile_rows],
                second_tile,
                jnp.zeros((tile_rows, width - 2 * tile_cols), jnp.float32),
            ],
            axis=1,
        )
        rest_block = jnp.concatenate([first_cols[tile_rows:], second_cols, trailing], axis=1)
        result = jnp.concatenate([first_block, second_block, rest_block], axis=0)
        result = result.reshape(NT, tile_rows, NT, tile_cols).transpose(0, 2, 1, 3)
    return result.reshape(NT, 1, NT, 1, tile_rows * tile_cols)


def solution(mesh):
    placed = (P(None, "row", None, "col", None),)
    return jax.shard_map(
        per_device,
        mesh=mesh,
        in_specs=placed,
        out_specs=P(None, "row", None, "col", None),
        check_vma=False,
    )
```

```python
import jax
import jax.numpy as jnp
from jax import lax
from jax.experimental import pallas as pl
from jax.experimental.pallas import tpu as pltpu
from jax.sharding import PartitionSpec as P

P_SIZE = 512
NT = 16


def bf16_gram(left_side, right_side):
    return lax.dot_general(
        left_side.astype(jnp.bfloat16),
        right_side.astype(jnp.bfloat16),
        (((1,), (1,)), ((), ())),
        preferred_element_type=jnp.float32,
    )


BLOCK = 128
GROUP = 4
EXACT = lax.Precision.HIGHEST


def exact_dot(left_side, right_side):
    return lax.dot_general(
        left_side, right_side, (((1,), (1,)), ((), ())),
        precision=EXACT, preferred_element_type=jnp.float32,
    )


def split_dot(narrow_side, right_side):
    parts = []
    remainder = right_side
    for _ in range(3):
        piece = lax.reduce_precision(remainder, exponent_bits=8, mantissa_bits=7)
        parts.append(piece.astype(jnp.bfloat16))
        remainder = remainder - piece
    narrow_side = narrow_side.astype(jnp.bfloat16)
    total = bf16_gram(narrow_side, parts[0])
    return total + (bf16_gram(narrow_side, parts[1]) + bf16_gram(narrow_side, parts[2]))


def factor_kernel(sym_ref, low_ref, inv_ref, work_ref, diag_ref, dinv_ref):
    size = sym_ref.shape[0]
    blocks = size // BLOCK
    work_ref[...] = sym_ref[...]
    low_ref[...] = jnp.zeros_like(low_ref)
    inv_ref[...] = jnp.zeros_like(inv_ref)
    rows = lax.broadcasted_iota(jnp.int32, (BLOCK, BLOCK), 0)
    lanes = lax.broadcasted_iota(jnp.int32, (BLOCK, BLOCK), 1)
    col_ids = lax.broadcasted_iota(jnp.int32, (BLOCK, 1), 0)
    row_ids = lax.broadcasted_iota(jnp.int32, (1, BLOCK), 1)
    eye = jnp.where(rows == lanes, 1.0, 0.0).astype(jnp.float32)
    for k in range(blocks):
        here = pl.ds(k * BLOCK, BLOCK)
        diag_ref[...] = jnp.zeros((BLOCK, BLOCK), jnp.float32)
        dinv_ref[...] = eye

        def pick_col(block, at):
            return jnp.sum(jnp.where(lanes == at, block, 0.0), axis=1, keepdims=True)

        def pick_row(block, at):
            return jnp.sum(jnp.where(rows == at, block, 0.0), axis=0, keepdims=True)

        def entry(vector, at):
            return jnp.sum(jnp.where(col_ids == at, vector, 0.0), axis=0, keepdims=True)

        group = GROUP

        def step(part, block):
            base = group * part
            c_cols = []
            c_rows = []
            scales = []
            raw_cols = []
            for g in range(group):
                at = base + g
                v_col = pick_col(block, at)
                v_row = pick_row(block, at)
                for i in range(g):
                    weight = entry(raw_cols[i], at) * scales[i]
                    v_col = v_col - c_cols[i] * weight
                    v_row = v_row - c_rows[i] * weight
                root = jnp.sqrt(entry(v_col, at))
                scale = 1.0 / root
                c_cols.append(jnp.where(col_ids > at, v_col * scale, jnp.where(col_ids == at, root, 0.0)))
                c_rows.append(jnp.where(row_ids > at, v_row * scale, jnp.where(row_ids == at, root, 0.0)))
                scales.append(scale)
                raw_cols.append(v_col)
            low = diag_ref[...]
            inverse = dinv_ref[...]
            for g in range(group):
                at = base + g
                low = jnp.where(lanes == at, c_cols[g], low)
                shift = c_cols[g] * scales[g] - jnp.where(col_ids == at, scales[g], 0.0)
                inverse = inverse - shift * pick_row(inverse, at)
                block = block - c_cols[g] * c_rows[g]
            diag_ref[...] = low
            dinv_ref[...] = inverse
            return block

        lax.fori_loop(0, BLOCK // group, step, work_ref[here, here], unroll=1)
        low_ref[here, here] = diag_ref[...]
        inv_ref[here, here] = dinv_ref[...]
        if k + 1 < blocks:
            rest = pl.ds((k + 1) * BLOCK, size - (k + 1) * BLOCK)
            panel = exact_dot(work_ref[rest, here], dinv_ref[...])
            low_ref[rest, here] = panel
            work_ref[rest, rest] = work_ref[rest, rest] - exact_dot(panel, panel)
    for i in range(1, blocks):
        at_i = pl.ds(i * BLOCK, BLOCK)
        for k in range(i):
            at_k = pl.ds(k * BLOCK, BLOCK)
            total = jnp.zeros((BLOCK, BLOCK), jnp.float32)
            for m in range(k, i):
                at_m = pl.ds(m * BLOCK, BLOCK)
                total = total + jnp.dot(
                    low_ref[at_i, at_m], inv_ref[at_m, at_k],
                    precision=EXACT, preferred_element_type=jnp.float32,
                )
            inv_ref[at_i, at_k] = -jnp.dot(
                inv_ref[at_i, at_i], total,
                precision=EXACT, preferred_element_type=jnp.float32,
            )


def factor_and_inverse(sym):
    size = sym.shape[0]
    return pl.pallas_call(
        factor_kernel,
        out_shape=(
            jax.ShapeDtypeStruct((size, size), jnp.float32),
            jax.ShapeDtypeStruct((size, size), jnp.float32),
        ),
        in_specs=[pl.BlockSpec(memory_space=pltpu.VMEM)],
        out_specs=(
            pl.BlockSpec(memory_space=pltpu.VMEM),
            pl.BlockSpec(memory_space=pltpu.VMEM),
        ),
        scratch_shapes=[
            pltpu.VMEM((size, size), jnp.float32),
            pltpu.VMEM((BLOCK, BLOCK), jnp.float32),
            pltpu.VMEM((BLOCK, BLOCK), jnp.float32),
        ],
    )(sym)


def per_device(kernel):
    row_count = lax.axis_size("row")
    col_count = lax.axis_size("col")
    tile_rows = P_SIZE // row_count
    tile_cols = P_SIZE // col_count
    row_index = lax.axis_index("row")
    column_index = lax.axis_index("col")
    tiles = kernel.reshape(NT, NT, tile_rows, tile_cols)
    local = tiles.transpose(0, 2, 1, 3).reshape(NT * tile_rows, NT * tile_cols)

    with jax.named_scope("gather_inputs"):
        band = lax.all_gather(local[:, : 2 * tile_cols], "col", axis=0)
        band = band.reshape(col_count, NT * tile_rows, 2, tile_cols)
        band = band.transpose(1, 2, 0, 3).reshape(NT * tile_rows, 2 * P_SIZE)
        own_rows = band[tile_rows:]
        corner = lax.all_gather(band[:tile_rows, :P_SIZE], "row", axis=0, tiled=True)
        corner = corner.astype(jnp.float32)
        top = jnp.concatenate([band[: 2 * tile_rows], local[: 2 * tile_rows, 2 * tile_cols :]], axis=1)
        top = lax.all_gather(top, "row", axis=0)
        top = top.reshape(row_count, 2, tile_rows, top.shape[-1]).transpose(1, 0, 2, 3)
        top = top.reshape(2 * P_SIZE, top.shape[-1])
        corners = jnp.stack([top[P_SIZE:, :P_SIZE], top[P_SIZE : 2 * P_SIZE, P_SIZE : 2 * P_SIZE]])
        own_second = lax.dynamic_slice_in_dim(top, P_SIZE + column_index * tile_cols, tile_cols, 1)
        col_rows = jnp.concatenate([own_second, top[:, 2 * P_SIZE :]], axis=1).T

    with jax.named_scope("first_panel"):
        first_factor, first_inverse = factor_and_inverse(0.5 * (corner + corner.T))
        own_count = (NT - 1) * tile_rows
        col_total = (NT - 1) * tile_cols
        stacked = jnp.concatenate(
            [corners[0], own_rows[:, :P_SIZE], col_rows[:, :P_SIZE]], axis=0
        )
        solved = split_dot(stacked, first_inverse)
        next_rows = solved[:P_SIZE].astype(jnp.bfloat16)
        first_own = solved[P_SIZE : P_SIZE + own_count]
        first_col = solved[P_SIZE + own_count :]

    with jax.named_scope("second_panel"):
        second_corner = corners[1].astype(jnp.float32) - bf16_gram(next_rows, next_rows)
        second_factor, second_inverse = factor_and_inverse(0.5 * (second_corner + second_corner.T))
        own_below = own_rows[tile_rows:, P_SIZE:].astype(jnp.float32) - bf16_gram(first_own[tile_rows:], next_rows)
        col_below = col_rows[tile_cols:, P_SIZE:].astype(jnp.float32) - bf16_gram(first_col[tile_cols:], next_rows)
        solved = exact_dot(jnp.concatenate([own_below, col_below], axis=0), second_inverse)
        second_own = solved[: own_count - tile_rows]
        second_col = solved[own_count - tile_rows :]

    with jax.named_scope("trailing_update"):
        trailing = local[2 * tile_rows :, 2 * tile_cols :]
        trailing = trailing.astype(jnp.float32) - bf16_gram(
            first_own[tile_rows:], first_col[tile_cols:]
        )
        trailing = trailing - bf16_gram(second_own, second_col)

    with jax.named_scope("assemble"):
        start_row = row_index * tile_rows
        start_col = column_index * tile_cols
        first_corner = lax.dynamic_slice(first_factor, (start_row, start_col), (tile_rows, tile_cols))
        second_tile = lax.dynamic_slice(second_factor, (start_row, start_col), (tile_rows, tile_cols))
        first_cols = lax.dynamic_slice_in_dim(first_own, start_col, tile_cols, 1)
        second_cols = lax.dynamic_slice_in_dim(second_own, start_col, tile_cols, 1)
        width = NT * tile_cols
        first_block = jnp.concatenate(
            [first_corner, jnp.zeros((tile_rows, width - tile_cols), jnp.float32)], axis=1
        )
        second_block = jnp.concatenate(
            [
                first_cols[:tile_rows],
                second_tile,
                jnp.zeros((tile_rows, width - 2 * tile_cols), jnp.float32),
            ],
            axis=1,
        )
        rest_block = jnp.concatenate([first_cols[tile_rows:], second_cols, trailing], axis=1)
        result = jnp.concatenate([first_block, second_block, rest_block], axis=0)
        result = result.reshape(NT, tile_rows, NT, tile_cols).transpose(0, 2, 1, 3)
    return result.reshape(NT, 1, NT, 1, tile_rows * tile_cols)


def solution(mesh):
    placed = (P(None, "row", None, "col", None),)
    return jax.shard_map(
        per_device,
        mesh=mesh,
        in_specs=placed,
        out_specs=P(None, "row", None, "col", None),
        check_vma=False,
    )
```

```python
import jax
import jax.numpy as jnp
from jax import lax
from jax.experimental import pallas as pl
from jax.experimental.pallas import tpu as pltpu
from jax.sharding import PartitionSpec as P

P_SIZE = 512
NT = 16


def bf16_gram(left_side, right_side):
    return lax.dot_general(
        left_side.astype(jnp.bfloat16),
        right_side.astype(jnp.bfloat16),
        (((1,), (1,)), ((), ())),
        preferred_element_type=jnp.float32,
    )


BLOCK = 128
GROUP = 4
EXACT = lax.Precision.HIGHEST


def exact_dot(left_side, right_side):
    return lax.dot_general(
        left_side, right_side, (((1,), (1,)), ((), ())),
        precision=EXACT, preferred_element_type=jnp.float32,
    )


def split_dot(narrow_side, right_side):
    parts = []
    remainder = right_side
    for _ in range(3):
        piece = lax.reduce_precision(remainder, exponent_bits=8, mantissa_bits=7)
        parts.append(piece.astype(jnp.bfloat16))
        remainder = remainder - piece
    size = right_side.shape[0]
    wide = bf16_gram(narrow_side.astype(jnp.bfloat16), jnp.concatenate(parts, axis=0))
    return wide[:, :size] + (wide[:, size : 2 * size] + wide[:, 2 * size :])


def factor_kernel(sym_ref, low_ref, inv_ref, work_ref, diag_ref, dinv_ref):
    size = sym_ref.shape[0]
    blocks = size // BLOCK
    work_ref[...] = sym_ref[...]
    low_ref[...] = jnp.zeros_like(low_ref)
    inv_ref[...] = jnp.zeros_like(inv_ref)
    rows = lax.broadcasted_iota(jnp.int32, (BLOCK, BLOCK), 0)
    lanes = lax.broadcasted_iota(jnp.int32, (BLOCK, BLOCK), 1)
    col_ids = lax.broadcasted_iota(jnp.int32, (BLOCK, 1), 0)
    row_ids = lax.broadcasted_iota(jnp.int32, (1, BLOCK), 1)
    eye = jnp.where(rows == lanes, 1.0, 0.0).astype(jnp.float32)
    for k in range(blocks):
        here = pl.ds(k * BLOCK, BLOCK)
        diag_ref[...] = jnp.zeros((BLOCK, BLOCK), jnp.float32)
        dinv_ref[...] = eye

        def pick_col(block, at):
            return jnp.sum(jnp.where(lanes == at, block, 0.0), axis=1, keepdims=True)

        def pick_row(block, at):
            return jnp.sum(jnp.where(rows == at, block, 0.0), axis=0, keepdims=True)

        def entry(vector, at):
            return jnp.sum(jnp.where(col_ids == at, vector, 0.0), axis=0, keepdims=True)

        group = GROUP

        def step(part, block):
            base = group * part
            c_cols = []
            c_rows = []
            scales = []
            raw_cols = []
            for g in range(group):
                at = base + g
                v_col = pick_col(block, at)
                v_row = pick_row(block, at)
                for i in range(g):
                    weight = entry(raw_cols[i], at) * scales[i]
                    v_col = v_col - c_cols[i] * weight
                    v_row = v_row - c_rows[i] * weight
                root = jnp.sqrt(entry(v_col, at))
                scale = 1.0 / root
                c_cols.append(jnp.where(col_ids > at, v_col * scale, jnp.where(col_ids == at, root, 0.0)))
                c_rows.append(jnp.where(row_ids > at, v_row * scale, jnp.where(row_ids == at, root, 0.0)))
                scales.append(scale)
                raw_cols.append(v_col)
            low = diag_ref[...]
            inverse = dinv_ref[...]
            for g in range(group):
                at = base + g
                low = jnp.where(lanes == at, c_cols[g], low)
                shift = c_cols[g] * scales[g] - jnp.where(col_ids == at, scales[g], 0.0)
                inverse = inverse - shift * pick_row(inverse, at)
                block = block - c_cols[g] * c_rows[g]
            diag_ref[...] = low
            dinv_ref[...] = inverse
            return block

        lax.fori_loop(0, BLOCK // group, step, work_ref[here, here], unroll=1)
        low_ref[here, here] = diag_ref[...]
        inv_ref[here, here] = dinv_ref[...]
        if k + 1 < blocks:
            rest = pl.ds((k + 1) * BLOCK, size - (k + 1) * BLOCK)
            panel = exact_dot(work_ref[rest, here], dinv_ref[...])
            low_ref[rest, here] = panel
            work_ref[rest, rest] = work_ref[rest, rest] - exact_dot(panel, panel)
    for i in range(1, blocks):
        at_i = pl.ds(i * BLOCK, BLOCK)
        for k in range(i):
            at_k = pl.ds(k * BLOCK, BLOCK)
            total = jnp.zeros((BLOCK, BLOCK), jnp.float32)
            for m in range(k, i):
                at_m = pl.ds(m * BLOCK, BLOCK)
                total = total + jnp.dot(
                    low_ref[at_i, at_m], inv_ref[at_m, at_k],
                    precision=EXACT, preferred_element_type=jnp.float32,
                )
            inv_ref[at_i, at_k] = -jnp.dot(
                inv_ref[at_i, at_i], total,
                precision=EXACT, preferred_element_type=jnp.float32,
            )


def factor_and_inverse(sym):
    size = sym.shape[0]
    return pl.pallas_call(
        factor_kernel,
        out_shape=(
            jax.ShapeDtypeStruct((size, size), jnp.float32),
            jax.ShapeDtypeStruct((size, size), jnp.float32),
        ),
        in_specs=[pl.BlockSpec(memory_space=pltpu.VMEM)],
        out_specs=(
            pl.BlockSpec(memory_space=pltpu.VMEM),
            pl.BlockSpec(memory_space=pltpu.VMEM),
        ),
        scratch_shapes=[
            pltpu.VMEM((size, size), jnp.float32),
            pltpu.VMEM((BLOCK, BLOCK), jnp.float32),
            pltpu.VMEM((BLOCK, BLOCK), jnp.float32),
        ],
    )(sym)


def per_device(kernel):
    row_count = lax.axis_size("row")
    col_count = lax.axis_size("col")
    tile_rows = P_SIZE // row_count
    tile_cols = P_SIZE // col_count
    row_index = lax.axis_index("row")
    column_index = lax.axis_index("col")
    tiles = kernel.reshape(NT, NT, tile_rows, tile_cols)
    local = tiles.transpose(0, 2, 1, 3).reshape(NT * tile_rows, NT * tile_cols)

    with jax.named_scope("gather_inputs"):
        band = lax.all_gather(local[:, : 2 * tile_cols], "col", axis=0)
        band = band.reshape(col_count, NT * tile_rows, 2, tile_cols)
        band = band.transpose(1, 2, 0, 3).reshape(NT * tile_rows, 2 * P_SIZE)
        own_rows = band[tile_rows:]
        corner = lax.all_gather(band[:tile_rows, :P_SIZE], "row", axis=0, tiled=True)
        corner = corner.astype(jnp.float32)
        top = jnp.concatenate([band[: 2 * tile_rows], local[: 2 * tile_rows, 2 * tile_cols :]], axis=1)
        top = lax.all_gather(top, "row", axis=0)
        top = top.reshape(row_count, 2, tile_rows, top.shape[-1]).transpose(1, 0, 2, 3)
        top = top.reshape(2 * P_SIZE, top.shape[-1])
        corners = jnp.stack([top[P_SIZE:, :P_SIZE], top[P_SIZE : 2 * P_SIZE, P_SIZE : 2 * P_SIZE]])
        own_second = lax.dynamic_slice_in_dim(top, P_SIZE + column_index * tile_cols, tile_cols, 1)
        col_rows = jnp.concatenate([own_second, top[:, 2 * P_SIZE :]], axis=1).T

    with jax.named_scope("first_panel"):
        first_factor, first_inverse = factor_and_inverse(0.5 * (corner + corner.T))
        own_count = (NT - 1) * tile_rows
        col_total = (NT - 1) * tile_cols
        stacked = jnp.concatenate(
            [corners[0], own_rows[:, :P_SIZE], col_rows[:, :P_SIZE]], axis=0
        )
        solved = split_dot(stacked, first_inverse)
        next_rows = solved[:P_SIZE].astype(jnp.bfloat16)
        first_own = solved[P_SIZE : P_SIZE + own_count]
        first_col = solved[P_SIZE + own_count :]

    with jax.named_scope("second_panel"):
        second_corner = corners[1].astype(jnp.float32) - bf16_gram(next_rows, next_rows)
        second_factor, second_inverse = factor_and_inverse(0.5 * (second_corner + second_corner.T))
        own_below = own_rows[tile_rows:, P_SIZE:].astype(jnp.float32) - bf16_gram(first_own[tile_rows:], next_rows)
        col_below = col_rows[tile_cols:, P_SIZE:].astype(jnp.float32) - bf16_gram(first_col[tile_cols:], next_rows)
        solved = exact_dot(jnp.concatenate([own_below, col_below], axis=0), second_inverse)
        second_own = solved[: own_count - tile_rows]
        second_col = solved[own_count - tile_rows :]

    with jax.named_scope("trailing_update"):
        trailing = local[2 * tile_rows :, 2 * tile_cols :]
        trailing = trailing.astype(jnp.float32) - bf16_gram(
            first_own[tile_rows:], first_col[tile_cols:]
        )
        trailing = trailing - bf16_gram(second_own, second_col)

    with jax.named_scope("assemble"):
        start_row = row_index * tile_rows
        start_col = column_index * tile_cols
        first_corner = lax.dynamic_slice(first_factor, (start_row, start_col), (tile_rows, tile_cols))
        second_tile = lax.dynamic_slice(second_factor, (start_row, start_col), (tile_rows, tile_cols))
        first_cols = lax.dynamic_slice_in_dim(first_own, start_col, tile_cols, 1)
        second_cols = lax.dynamic_slice_in_dim(second_own, start_col, tile_cols, 1)
        width = NT * tile_cols
        first_block = jnp.concatenate(
            [first_corner, jnp.zeros((tile_rows, width - tile_cols), jnp.float32)], axis=1
        )
        second_block = jnp.concatenate(
            [
                first_cols[:tile_rows],
                second_tile,
                jnp.zeros((tile_rows, width - 2 * tile_cols), jnp.float32),
            ],
            axis=1,
        )
        rest_block = jnp.concatenate([first_cols[tile_rows:], second_cols, trailing], axis=1)
        result = jnp.concatenate([first_block, second_block, rest_block], axis=0)
        result = result.reshape(NT, tile_rows, NT, tile_cols).transpose(0, 2, 1, 3)
    return result.reshape(NT, 1, NT, 1, tile_rows * tile_cols)


def solution(mesh):
    placed = (P(None, "row", None, "col", None),)
    return jax.shard_map(
        per_device,
        mesh=mesh,
        in_specs=placed,
        out_specs=P(None, "row", None, "col", None),
        check_vma=False,
    )
```

```python
import jax
import jax.numpy as jnp
from jax import lax
from jax.experimental import pallas as pl
from jax.experimental.pallas import tpu as pltpu
from jax.sharding import PartitionSpec as P

P_SIZE = 512
NT = 16


def bf16_gram(left_side, right_side):
    return lax.dot_general(
        left_side.astype(jnp.bfloat16),
        right_side.astype(jnp.bfloat16),
        (((1,), (1,)), ((), ())),
        preferred_element_type=jnp.float32,
    )


BLOCK = 128
GROUP = 4
EXACT = lax.Precision.HIGHEST


def exact_dot(left_side, right_side):
    return lax.dot_general(
        left_side, right_side, (((1,), (1,)), ((), ())),
        precision=EXACT, preferred_element_type=jnp.float32,
    )


def split_dot(narrow_side, right_side):
    parts = []
    remainder = right_side
    for _ in range(3):
        piece = lax.reduce_precision(remainder, exponent_bits=8, mantissa_bits=7)
        parts.append(piece.astype(jnp.bfloat16))
        remainder = remainder - piece
    narrow_side = narrow_side.astype(jnp.bfloat16)
    total = bf16_gram(narrow_side, parts[0])
    return total + (bf16_gram(narrow_side, parts[1]) + bf16_gram(narrow_side, parts[2]))


def factor_kernel(sym_ref, low_ref, inv_ref, work_ref, diag_ref, dinv_ref):
    size = sym_ref.shape[0]
    blocks = size // BLOCK
    work_ref[...] = sym_ref[...]
    for i in range(blocks):
        for k in range(i + 1, blocks):
            upper = (pl.ds(i * BLOCK, BLOCK), pl.ds(k * BLOCK, BLOCK))
            low_ref[upper] = jnp.zeros((BLOCK, BLOCK), jnp.float32)
            inv_ref[upper] = jnp.zeros((BLOCK, BLOCK), jnp.float32)
    rows = lax.broadcasted_iota(jnp.int32, (BLOCK, BLOCK), 0)
    lanes = lax.broadcasted_iota(jnp.int32, (BLOCK, BLOCK), 1)
    col_ids = lax.broadcasted_iota(jnp.int32, (BLOCK, 1), 0)
    row_ids = lax.broadcasted_iota(jnp.int32, (1, BLOCK), 1)
    eye = jnp.where(rows == lanes, 1.0, 0.0).astype(jnp.float32)
    for k in range(blocks):
        here = pl.ds(k * BLOCK, BLOCK)
        diag_ref[...] = jnp.zeros((BLOCK, BLOCK), jnp.float32)
        dinv_ref[...] = eye

        def pick_col(block, at):
            return jnp.sum(jnp.where(lanes == at, block, 0.0), axis=1, keepdims=True)

        def pick_row(block, at):
            return jnp.sum(jnp.where(rows == at, block, 0.0), axis=0, keepdims=True)

        def entry(vector, at):
            return jnp.sum(jnp.where(col_ids == at, vector, 0.0), axis=0, keepdims=True)

        group = GROUP

        def step(part, block):
            base = group * part
            c_cols = []
            c_rows = []
            scales = []
            raw_cols = []
            for g in range(group):
                at = base + g
                v_col = pick_col(block, at)
                v_row = pick_row(block, at)
                for i in range(g):
                    weight = entry(raw_cols[i], at) * scales[i]
                    v_col = v_col - c_cols[i] * weight
                    v_row = v_row - c_rows[i] * weight
                root = jnp.sqrt(entry(v_col, at))
                scale = 1.0 / root
                c_cols.append(jnp.where(col_ids > at, v_col * scale, jnp.where(col_ids == at, root, 0.0)))
                c_rows.append(jnp.where(row_ids > at, v_row * scale, jnp.where(row_ids == at, root, 0.0)))
                scales.append(scale)
                raw_cols.append(v_col)
            low = diag_ref[...]
            inverse = dinv_ref[...]
            for g in range(group):
                at = base + g
                low = jnp.where(lanes == at, c_cols[g], low)
                shift = c_cols[g] * scales[g] - jnp.where(col_ids == at, scales[g], 0.0)
                inverse = inverse - shift * pick_row(inverse, at)
                block = block - c_cols[g] * c_rows[g]
            diag_ref[...] = low
            dinv_ref[...] = inverse
            return block

        lax.fori_loop(0, BLOCK // group, step, work_ref[here, here], unroll=1)
        low_ref[here, here] = diag_ref[...]
        inv_ref[here, here] = dinv_ref[...]
        if k + 1 < blocks:
            rest = pl.ds((k + 1) * BLOCK, size - (k + 1) * BLOCK)
            panel = exact_dot(work_ref[rest, here], dinv_ref[...])
            low_ref[rest, here] = panel
            work_ref[rest, rest] = work_ref[rest, rest] - exact_dot(panel, panel)
    for i in range(1, blocks):
        at_i = pl.ds(i * BLOCK, BLOCK)
        for k in range(i):
            at_k = pl.ds(k * BLOCK, BLOCK)
            total = jnp.zeros((BLOCK, BLOCK), jnp.float32)
            for m in range(k, i):
                at_m = pl.ds(m * BLOCK, BLOCK)
                total = total + jnp.dot(
                    low_ref[at_i, at_m], inv_ref[at_m, at_k],
                    precision=EXACT, preferred_element_type=jnp.float32,
                )
            inv_ref[at_i, at_k] = -jnp.dot(
                inv_ref[at_i, at_i], total,
                precision=EXACT, preferred_element_type=jnp.float32,
            )


def factor_and_inverse(sym):
    size = sym.shape[0]
    return pl.pallas_call(
        factor_kernel,
        out_shape=(
            jax.ShapeDtypeStruct((size, size), jnp.float32),
            jax.ShapeDtypeStruct((size, size), jnp.float32),
        ),
        in_specs=[pl.BlockSpec(memory_space=pltpu.VMEM)],
        out_specs=(
            pl.BlockSpec(memory_space=pltpu.VMEM),
            pl.BlockSpec(memory_space=pltpu.VMEM),
        ),
        scratch_shapes=[
            pltpu.VMEM((size, size), jnp.float32),
            pltpu.VMEM((BLOCK, BLOCK), jnp.float32),
            pltpu.VMEM((BLOCK, BLOCK), jnp.float32),
        ],
    )(sym)


def per_device(kernel):
    row_count = lax.axis_size("row")
    col_count = lax.axis_size("col")
    tile_rows = P_SIZE // row_count
    tile_cols = P_SIZE // col_count
    row_index = lax.axis_index("row")
    column_index = lax.axis_index("col")
    tiles = kernel.reshape(NT, NT, tile_rows, tile_cols)
    local = tiles.transpose(0, 2, 1, 3).reshape(NT * tile_rows, NT * tile_cols)

    with jax.named_scope("gather_inputs"):
        band = lax.all_gather(local[:, : 2 * tile_cols], "col", axis=0)
        band = band.reshape(col_count, NT * tile_rows, 2, tile_cols)
        band = band.transpose(1, 2, 0, 3).reshape(NT * tile_rows, 2 * P_SIZE)
        own_rows = band[tile_rows:]
        corner = lax.all_gather(band[:tile_rows, :P_SIZE], "row", axis=0, tiled=True)
        corner = corner.astype(jnp.float32)
        top = jnp.concatenate([band[: 2 * tile_rows], local[: 2 * tile_rows, 2 * tile_cols :]], axis=1)
        top = lax.all_gather(top, "row", axis=0)
        top = top.reshape(row_count, 2, tile_rows, top.shape[-1]).transpose(1, 0, 2, 3)
        top = top.reshape(2 * P_SIZE, top.shape[-1])
        corners = jnp.stack([top[P_SIZE:, :P_SIZE], top[P_SIZE : 2 * P_SIZE, P_SIZE : 2 * P_SIZE]])
        own_second = lax.dynamic_slice_in_dim(top, P_SIZE + column_index * tile_cols, tile_cols, 1)
        col_rows = jnp.concatenate([own_second, top[:, 2 * P_SIZE :]], axis=1).T

    with jax.named_scope("first_panel"):
        first_factor, first_inverse = factor_and_inverse(0.5 * (corner + corner.T))
        own_count = (NT - 1) * tile_rows
        col_total = (NT - 1) * tile_cols
        stacked = jnp.concatenate(
            [corners[0], own_rows[:, :P_SIZE], col_rows[:, :P_SIZE]], axis=0
        )
        solved = split_dot(stacked, first_inverse)
        next_rows = solved[:P_SIZE].astype(jnp.bfloat16)
        first_own = solved[P_SIZE : P_SIZE + own_count]
        first_col = solved[P_SIZE + own_count :]

    with jax.named_scope("second_panel"):
        second_corner = corners[1].astype(jnp.float32) - bf16_gram(next_rows, next_rows)
        second_factor, second_inverse = factor_and_inverse(0.5 * (second_corner + second_corner.T))
        own_below = own_rows[tile_rows:, P_SIZE:].astype(jnp.float32) - bf16_gram(first_own[tile_rows:], next_rows)
        col_below = col_rows[tile_cols:, P_SIZE:].astype(jnp.float32) - bf16_gram(first_col[tile_cols:], next_rows)
        solved = exact_dot(jnp.concatenate([own_below, col_below], axis=0), second_inverse)
        second_own = solved[: own_count - tile_rows]
        second_col = solved[own_count - tile_rows :]

    with jax.named_scope("trailing_update"):
        trailing = local[2 * tile_rows :, 2 * tile_cols :]
        trailing = trailing.astype(jnp.float32) - bf16_gram(
            first_own[tile_rows:], first_col[tile_cols:]
        )
        trailing = trailing - bf16_gram(second_own, second_col)

    with jax.named_scope("assemble"):
        start_row = row_index * tile_rows
        start_col = column_index * tile_cols
        first_corner = lax.dynamic_slice(first_factor, (start_row, start_col), (tile_rows, tile_cols))
        second_tile = lax.dynamic_slice(second_factor, (start_row, start_col), (tile_rows, tile_cols))
        first_cols = lax.dynamic_slice_in_dim(first_own, start_col, tile_cols, 1)
        second_cols = lax.dynamic_slice_in_dim(second_own, start_col, tile_cols, 1)
        width = NT * tile_cols
        first_block = jnp.concatenate(
            [first_corner, jnp.zeros((tile_rows, width - tile_cols), jnp.float32)], axis=1
        )
        second_block = jnp.concatenate(
            [
                first_cols[:tile_rows],
                second_tile,
                jnp.zeros((tile_rows, width - 2 * tile_cols), jnp.float32),
            ],
            axis=1,
        )
        rest_block = jnp.concatenate([first_cols[tile_rows:], second_cols, trailing], axis=1)
        result = jnp.concatenate([first_block, second_block, rest_block], axis=0)
        result = result.reshape(NT, tile_rows, NT, tile_cols).transpose(0, 2, 1, 3)
    return result.reshape(NT, 1, NT, 1, tile_rows * tile_cols)


def solution(mesh):
    placed = (P(None, "row", None, "col", None),)
    return jax.shard_map(
        per_device,
        mesh=mesh,
        in_specs=placed,
        out_specs=P(None, "row", None, "col", None),
        check_vma=False,
    )
```

```python
import jax
import jax.numpy as jnp
from jax import lax
from jax.experimental import pallas as pl
from jax.experimental.pallas import tpu as pltpu
from jax.sharding import PartitionSpec as P

P_SIZE = 512
NT = 16


def bf16_gram(left_side, right_side):
    return lax.dot_general(
        left_side.astype(jnp.bfloat16),
        right_side.astype(jnp.bfloat16),
        (((1,), (1,)), ((), ())),
        preferred_element_type=jnp.float32,
    )


BLOCK = 128
GROUP = 4
EXACT = lax.Precision.HIGHEST


def exact_dot(left_side, right_side):
    return lax.dot_general(
        left_side, right_side, (((1,), (1,)), ((), ())),
        precision=EXACT, preferred_element_type=jnp.float32,
    )


def split_dot(narrow_side, right_side):
    parts = []
    remainder = right_side
    for _ in range(3):
        piece = lax.reduce_precision(remainder, exponent_bits=8, mantissa_bits=7)
        parts.append(piece.astype(jnp.bfloat16))
        remainder = remainder - piece
    narrow_side = narrow_side.astype(jnp.bfloat16)
    total = bf16_gram(narrow_side, parts[0])
    return total + (bf16_gram(narrow_side, parts[1]) + bf16_gram(narrow_side, parts[2]))


def factor_kernel(sym_ref, low_ref, inv_ref, work_ref, diag_ref, dinv_ref):
    size = sym_ref.shape[0]
    blocks = size // BLOCK
    work_ref[...] = sym_ref[...]
    low_ref[...] = jnp.zeros_like(low_ref)
    inv_ref[...] = jnp.zeros_like(inv_ref)
    rows = lax.broadcasted_iota(jnp.int32, (BLOCK, BLOCK), 0)
    lanes = lax.broadcasted_iota(jnp.int32, (BLOCK, BLOCK), 1)
    col_ids = lax.broadcasted_iota(jnp.int32, (BLOCK, 1), 0)
    row_ids = lax.broadcasted_iota(jnp.int32, (1, BLOCK), 1)
    eye = jnp.where(rows == lanes, 1.0, 0.0).astype(jnp.float32)
    for k in range(blocks):
        here = pl.ds(k * BLOCK, BLOCK)
        diag_ref[...] = jnp.zeros((BLOCK, BLOCK), jnp.float32)
        dinv_ref[...] = eye

        def pick_col(block, at):
            return jnp.sum(jnp.where(lanes == at, block, 0.0), axis=1, keepdims=True)

        def pick_row(block, at):
            return jnp.sum(jnp.where(rows == at, block, 0.0), axis=0, keepdims=True)

        def entry(vector, at):
            return jnp.sum(jnp.where(col_ids == at, vector, 0.0), axis=0, keepdims=True)

        group = GROUP

        def step(part, block):
            base = group * part
            c_cols = []
            c_rows = []
            scales = []
            raw_cols = []
            for g in range(group):
                at = base + g
                v_col = pick_col(block, at)
                v_row = pick_row(block, at)
                for i in range(g):
                    weight = entry(raw_cols[i], at) * scales[i]
                    v_col = v_col - c_cols[i] * weight
                    v_row = v_row - c_rows[i] * weight
                root = jnp.sqrt(entry(v_col, at))
                scale = 1.0 / root
                c_cols.append(jnp.where(col_ids > at, v_col * scale, jnp.where(col_ids == at, root, 0.0)))
                c_rows.append(jnp.where(row_ids > at, v_row * scale, jnp.where(row_ids == at, root, 0.0)))
                scales.append(scale)
                raw_cols.append(v_col)
            low = diag_ref[...]
            inverse = dinv_ref[...]
            for g in range(group):
                at = base + g
                low = jnp.where(lanes == at, c_cols[g], low)
                shift = c_cols[g] * scales[g] - jnp.where(col_ids == at, scales[g], 0.0)
                inverse = inverse - shift * pick_row(inverse, at)
                block = block - c_cols[g] * c_rows[g]
            diag_ref[...] = low
            dinv_ref[...] = inverse
            return block

        lax.fori_loop(0, BLOCK // group, step, work_ref[here, here], unroll=2)
        low_ref[here, here] = diag_ref[...]
        inv_ref[here, here] = dinv_ref[...]
        if k + 1 < blocks:
            rest = pl.ds((k + 1) * BLOCK, size - (k + 1) * BLOCK)
            panel = exact_dot(work_ref[rest, here], dinv_ref[...])
            low_ref[rest, here] = panel
            work_ref[rest, rest] = work_ref[rest, rest] - exact_dot(panel, panel)
    for i in range(1, blocks):
        at_i = pl.ds(i * BLOCK, BLOCK)
        for k in range(i):
            at_k = pl.ds(k * BLOCK, BLOCK)
            total = jnp.zeros((BLOCK, BLOCK), jnp.float32)
            for m in range(k, i):
                at_m = pl.ds(m * BLOCK, BLOCK)
                total = total + jnp.dot(
                    low_ref[at_i, at_m], inv_ref[at_m, at_k],
                    precision=EXACT, preferred_element_type=jnp.float32,
                )
            inv_ref[at_i, at_k] = -jnp.dot(
                inv_ref[at_i, at_i], total,
                precision=EXACT, preferred_element_type=jnp.float32,
            )


def factor_and_inverse(sym):
    size = sym.shape[0]
    return pl.pallas_call(
        factor_kernel,
        out_shape=(
            jax.ShapeDtypeStruct((size, size), jnp.float32),
            jax.ShapeDtypeStruct((size, size), jnp.float32),
        ),
        in_specs=[pl.BlockSpec(memory_space=pltpu.VMEM)],
        out_specs=(
            pl.BlockSpec(memory_space=pltpu.VMEM),
            pl.BlockSpec(memory_space=pltpu.VMEM),
        ),
        scratch_shapes=[
            pltpu.VMEM((size, size), jnp.float32),
            pltpu.VMEM((BLOCK, BLOCK), jnp.float32),
            pltpu.VMEM((BLOCK, BLOCK), jnp.float32),
        ],
    )(sym)


def per_device(kernel):
    row_count = lax.axis_size("row")
    col_count = lax.axis_size("col")
    tile_rows = P_SIZE // row_count
    tile_cols = P_SIZE // col_count
    row_index = lax.axis_index("row")
    column_index = lax.axis_index("col")
    tiles = kernel.reshape(NT, NT, tile_rows, tile_cols)
    local = tiles.transpose(0, 2, 1, 3).reshape(NT * tile_rows, NT * tile_cols)

    with jax.named_scope("gather_inputs"):
        band = lax.all_gather(local[:, : 2 * tile_cols], "col", axis=0)
        band = band.reshape(col_count, NT * tile_rows, 2, tile_cols)
        band = band.transpose(1, 2, 0, 3).reshape(NT * tile_rows, 2 * P_SIZE)
        own_rows = band[tile_rows:]
        corner = lax.all_gather(band[:tile_rows, :P_SIZE], "row", axis=0, tiled=True)
        corner = corner.astype(jnp.float32)
        top = jnp.concatenate([band[: 2 * tile_rows], local[: 2 * tile_rows, 2 * tile_cols :]], axis=1)
        top = lax.all_gather(top, "row", axis=0)
        top = top.reshape(row_count, 2, tile_rows, top.shape[-1]).transpose(1, 0, 2, 3)
        top = top.reshape(2 * P_SIZE, top.shape[-1])
        corners = jnp.stack([top[P_SIZE:, :P_SIZE], top[P_SIZE : 2 * P_SIZE, P_SIZE : 2 * P_SIZE]])
        own_second = lax.dynamic_slice_in_dim(top, P_SIZE + column_index * tile_cols, tile_cols, 1)
        col_rows = jnp.concatenate([own_second, top[:, 2 * P_SIZE :]], axis=1).T

    with jax.named_scope("first_panel"):
        first_factor, first_inverse = factor_and_inverse(0.5 * (corner + corner.T))
        own_count = (NT - 1) * tile_rows
        col_total = (NT - 1) * tile_cols
        stacked = jnp.concatenate(
            [corners[0], own_rows[:, :P_SIZE], col_rows[:, :P_SIZE]], axis=0
        )
        solved = split_dot(stacked, first_inverse)
        next_rows = solved[:P_SIZE].astype(jnp.bfloat16)
        first_own = solved[P_SIZE : P_SIZE + own_count]
        first_col = solved[P_SIZE + own_count :]

    with jax.named_scope("second_panel"):
        second_corner = corners[1].astype(jnp.float32) - bf16_gram(next_rows, next_rows)
        second_factor, second_inverse = factor_and_inverse(0.5 * (second_corner + second_corner.T))
        own_below = own_rows[tile_rows:, P_SIZE:].astype(jnp.float32) - bf16_gram(first_own[tile_rows:], next_rows)
        col_below = col_rows[tile_cols:, P_SIZE:].astype(jnp.float32) - bf16_gram(first_col[tile_cols:], next_rows)
        solved = exact_dot(jnp.concatenate([own_below, col_below], axis=0), second_inverse)
        second_own = solved[: own_count - tile_rows]
        second_col = solved[own_count - tile_rows :]

    with jax.named_scope("trailing_update"):
        trailing = local[2 * tile_rows :, 2 * tile_cols :]
        trailing = trailing.astype(jnp.float32) - bf16_gram(
            first_own[tile_rows:], first_col[tile_cols:]
        )
        trailing = trailing - bf16_gram(second_own, second_col)

    with jax.named_scope("assemble"):
        start_row = row_index * tile_rows
        start_col = column_index * tile_cols
        first_corner = lax.dynamic_slice(first_factor, (start_row, start_col), (tile_rows, tile_cols))
        second_tile = lax.dynamic_slice(second_factor, (start_row, start_col), (tile_rows, tile_cols))
        first_cols = lax.dynamic_slice_in_dim(first_own, start_col, tile_cols, 1)
        second_cols = lax.dynamic_slice_in_dim(second_own, start_col, tile_cols, 1)
        width = NT * tile_cols
        first_block = jnp.concatenate(
            [first_corner, jnp.zeros((tile_rows, width - tile_cols), jnp.float32)], axis=1
        )
        second_block = jnp.concatenate(
            [
                first_cols[:tile_rows],
                second_tile,
                jnp.zeros((tile_rows, width - 2 * tile_cols), jnp.float32),
            ],
            axis=1,
        )
        rest_block = jnp.concatenate([first_cols[tile_rows:], second_cols, trailing], axis=1)
        result = jnp.concatenate([first_block, second_block, rest_block], axis=0)
        result = result.reshape(NT, tile_rows, NT, tile_cols).transpose(0, 2, 1, 3)
    return result.reshape(NT, 1, NT, 1, tile_rows * tile_cols)


def solution(mesh):
    placed = (P(None, "row", None, "col", None),)
    return jax.shard_map(
        per_device,
        mesh=mesh,
        in_specs=placed,
        out_specs=P(None, "row", None, "col", None),
        check_vma=False,
    )
```
